128 devices in a mesh: tm: 8 (over x, core), batch: 16 (over y, z).
Axes of the slice: x: 4, y: 4, z: 4, core: 2. Of those that a mesh axis runs over, the one named last changes fastest.
Arguments:
- initial_state: float32 [4096, 256], P('batch'), may hold values from -6 to 6
- increments: float32 [64, 4096, 256], P('tm', 'batch'), may hold values from -1.5 to 1.5
- cotangents: float32 [64, 4096, 256], P('tm', 'batch'), may hold values from -1.5 to 1.5
- drift_inner: bfloat16 [256, 1024], replicated, may hold values from -0.375 to 0.375
- drift_hidden: float32 [1024], replicated, may hold values from -3 to 3
- drift_outer: bfloat16 [1024, 256], replicated, may hold values from -0.1875 to 0.1875
- drift_offset: float32 [256], replicated, may hold values from -3 to 3
- noise_inner: bfloat16 [256, 1024], replicated, may hold values from -0.375 to 0.375
- noise_hidden: float32 [1024], replicated, may hold values from -3 to 3
- noise_outer: bfloat16 [1024, 256], replicated, may hold values from -0.1875 to 0.1875
- noise_offset: float32 [256], replicated, may hold values from -4 to 4
Outputs:
- states: float32 [64, 4096, 256], P('tm', 'batch')
- adjoints: float32 [64, 4096, 256], P('tm', 'batch')
- drift_inner_grad: float32 [256, 1024], replicated
- drift_hidden_grad: float32 [1024], replicated
- drift_outer_grad: float32 [1024, 256], replicated
- drift_offset_grad: float32 [256], replicated
- noise_inner_grad: float32 [256, 1024], replicated
- noise_hidden_grad: float32 [1024], replicated
- noise_outer_grad: float32 [1024, 256], replicated
- noise_offset_grad: float32 [256], replicated
The draws below stay inside these ranges and needn't reach their ends.
All inputs are finite; a program needn't handle non-finite values.
Results may differ from the reference program's by a relative error of at most 0.0095.
Values sent between devices are 32-bit elements; how exact they have to be, the bound alone decides.
A program may use at most 128 MiB of HBM per device.

```python
import math
import jax
import jax.numpy as jnp
from jax import lax

L = 256
H = 1024
STEPS = 64
BATCH = 4096


def block_scale(own_key, shape, pieces, smallest, largest):
    def one(dim, blocks):
        draws = jax.random.uniform(jax.random.fold_in(jax.random.fold_in(own_key, 6), dim), (blocks,), jnp.float32, smallest / len(pieces), largest / len(pieces))
        return jnp.repeat(jnp.exp(draws), shape[dim] // blocks).reshape((-1,) + (1,) * (len(shape) - dim - 1))

    loudness = one(*pieces[0])
    for cut in pieces[1:]:
        loudness = loudness * one(*cut)
    return loudness


def scatter_about(stream_key, dims, deviation, most, pieces=(), held_as=jnp.bfloat16):
    array = jax.random.normal(stream_key, dims, jnp.float32) * deviation
    if len(pieces) > 0:
        array = block_scale(stream_key, dims, pieces, -0.22, 0.18) * array
    return jnp.clip(array, min=-most, max=most).astype(held_as)


def setup_inputs(seed: int = 0) -> dict:
    seeds = jax.random.split(jax.random.key(seed), 12)
    initial_state = scatter_about(seeds[0], (BATCH, L), 1.0, 6.0, ((0, 16),), jnp.float32)
    increments = scatter_about(seeds[1], (STEPS, BATCH, L), 0.224, 1.5, ((0, 8), (1, 16)), jnp.float32)
    cotangents = scatter_about(seeds[2], (STEPS, BATCH, L), 0.25, 1.5, ((0, 8), (1, 16)), jnp.float32)
    drift_inner = scatter_about(seeds[3], (L, H), L ** -0.5, 0.375)
    drift_hidden = scatter_about(seeds[4], (H,), 0.5, 3.0, (), jnp.float32)
    drift_outer = scatter_about(seeds[5], (H, L), H ** -0.5, 0.1875)
    drift_offset = scatter_about(seeds[6], (L,), 0.5, 3.0, (), jnp.float32)
    noise_inner = scatter_about(seeds[7], (L, H), L ** -0.5, 0.375)
    noise_hidden = scatter_about(seeds[8], (H,), 0.5, 3.0, (), jnp.float32)
    noise_outer = scatter_about(seeds[9], (H, L), H ** -0.5, 0.1875)
    noise_offset = scatter_about(seeds[10], (L,), 1.0, 4.0, (), jnp.float32)
    return {"initial_state": initial_state, "increments": increments, "cotangents": cotangents, "drift_inner": drift_inner, "drift_hidden": drift_hidden, "drift_outer": drift_outer, "drift_offset": drift_offset, "noise_inner": noise_inner, "noise_hidden": noise_hidden, "noise_outer": noise_outer, "noise_offset": noise_offset}


delta_time = 0.05

def matmul(left, right):
    return jnp.dot(left, right, preferred_element_type=jnp.float32)

def matmul_transposed(left, right):
    return lax.dot_general(left, right, (((1,), (1,)), ((), ())), preferred_element_type=jnp.float32)

def matmul_rows(left, right):
    return lax.dot_general(left, right, (((0,), (0,)), ((), ())), preferred_element_type=jnp.float32)

def advance(state, noise, params):
    drift_inner, drift_hidden, drift_outer, drift_offset, noise_inner, noise_hidden, noise_outer, noise_offset = params
    state_low = state.astype(jnp.bfloat16)
    hidden_drift = jnp.tanh(matmul(state_low, drift_inner) + drift_hidden).astype(jnp.bfloat16)
    hidden_noise = jnp.tanh(matmul(state_low, noise_inner) + noise_hidden).astype(jnp.bfloat16)
    drift = matmul(hidden_drift, drift_outer) + drift_offset
    spread = jax.nn.sigmoid(matmul(hidden_noise, noise_outer) + noise_offset)
    return (state + delta_time * drift + spread * noise, (state_low, hidden_drift, hidden_noise, spread))

def retreat(adjoint_next, state, noise, params):
    drift_inner, drift_hidden, drift_outer, drift_offset, noise_inner, noise_hidden, noise_outer, noise_offset = params
    unused, saved = advance(state, noise, params)
    state_low, hidden_drift, hidden_noise, spread = saved
    drift_grad = delta_time * adjoint_next
    noise_grad = adjoint_next * noise * spread * (1.0 - spread)
    drift_low = drift_grad.astype(jnp.bfloat16)
    noise_low = noise_grad.astype(jnp.bfloat16)
    back_drift = matmul_transposed(drift_low, drift_outer) * (1.0 - jnp.square(hidden_drift.astype(jnp.float32)))
    back_noise = matmul_transposed(noise_low, noise_outer) * (1.0 - jnp.square(hidden_noise.astype(jnp.float32)))
    back_drift_low = back_drift.astype(jnp.bfloat16)
    back_noise_low = back_noise.astype(jnp.bfloat16)
    adjoint = adjoint_next + matmul_transposed(back_drift_low, drift_inner) + matmul_transposed(back_noise_low, noise_inner)
    grads = (matmul_rows(state_low, back_drift_low), lax.optimization_barrier(jnp.sum(back_drift, 0)), matmul_rows(hidden_drift, drift_low), lax.optimization_barrier(jnp.sum(drift_grad, 0)), matmul_rows(state_low, back_noise_low), lax.optimization_barrier(jnp.sum(back_noise, 0)), matmul_rows(hidden_noise, noise_low), lax.optimization_barrier(jnp.sum(noise_grad, 0)))
    return (adjoint, grads)

def squares(grads):
    total = jnp.sum(jnp.square(grads[0]))
    for entry in grads[1:]:
        total = total + jnp.sum(jnp.square(entry))
    return total

def clip_factor(total):
    limit = 0.5 * math.sqrt(4 * L * H + 2 * H + 2 * L)
    return jnp.minimum(1.0, limit / jnp.sqrt(total))

def reference(initial_state, increments, cotangents, drift_inner, drift_hidden, drift_outer, drift_offset, noise_inner, noise_hidden, noise_outer, noise_offset):
    params = (drift_inner, drift_hidden, drift_outer, drift_offset, noise_inner, noise_hidden, noise_outer, noise_offset)

    def forward(state, noise):
        following, unused = advance(state, noise, params)
        return (following, (state, following))
    final, (entries, states) = lax.scan(forward, initial_state, increments)
    blank = tuple((jnp.zeros(p.shape, jnp.float32) for p in params))

    def backward(carry, inputs):
        adjoint_next, totals = carry
        entry, noise, cotangent = inputs
        adjoint, grads = retreat(adjoint_next + cotangent, entry, noise, params)
        totals = tuple((a + b for a, b in zip(totals, grads)))
        return ((adjoint, totals), adjoint)
    (unused, totals), adjoints = lax.scan(backward, (jnp.zeros_like(initial_state), blank), (entries, increments, cotangents), reverse=True)
    factor = clip_factor(squares(totals))
    return (states, adjoints, totals[0] * factor, totals[1] * factor, totals[2] * factor, totals[3] * factor, totals[4] * factor, totals[5] * factor, totals[6] * factor, totals[7] * factor)
```

```python
import math

import jax
import jax.numpy as jnp
from jax import lax
from jax.experimental import pallas as pl
from jax.experimental.pallas import tpu as pltpu
from jax.sharding import PartitionSpec as P

L = 256
H = 1024
CHUNKS = 4
delta_time = 0.05
F32 = jnp.float32
BF = jnp.bfloat16


def matmul(left, right):
    return jnp.dot(left, right, preferred_element_type=F32)


def matmul_rows(left, right):
    return lax.dot_general(left, right, (((0,), (0,)), ((), ())), preferred_element_type=F32)


def forward_kernel(start, noise, di, dh, do, dof, ni, nh, no, nof, states, q_out, u_out, v_out, s_out, carry):
    steps, rows, width = noise.shape
    chunk = H // CHUNKS

    @pl.when(pl.program_id(0) == 0)
    def _():
        carry[...] = start[...]

    def step(i, z):
        q = z.astype(BF)
        q_out[i] = q
        drift = noisy = None
        for c in range(CHUNKS):
            cols = slice(c * chunk, (c + 1) * chunk)
            u = jnp.tanh(matmul(q, di[:, cols]) + dh[:, cols]).astype(BF)
            v = jnp.tanh(matmul(q, ni[:, cols]) + nh[:, cols]).astype(BF)
            u_out[i, :, cols] = u
            v_out[i, :, cols] = v
            a, b = matmul(u, do[cols, :]), matmul(v, no[cols, :])
            drift = a if drift is None else drift + a
            noisy = b if noisy is None else noisy + b
        s = jax.nn.sigmoid(noisy + nof[...])
        s_out[i] = s
        z = z + delta_time * (drift + dof[...]) + s * noise[i]
        states[i] = z
        return z

    carry[...] = lax.fori_loop(0, steps, step, carry[...])


def backward_kernel(
    cot, noise, q_in, u_in, v_in, s_in, dot_, dit, not_, nit,
    adjoints, gdi, gdo, gni, gno, bias_hidden, bias_out,
    carry, pb_all, rb_all, fb_all, gb_all,
):
    steps, rows, width = noise.shape
    chunk = H // CHUNKS
    first = pl.program_id(0) == 0

    @pl.when(first)
    def _():
        carry[...] = jnp.zeros_like(carry)
        bias_hidden[...] = jnp.zeros_like(bias_hidden)
        bias_out[...] = jnp.zeros_like(bias_out)
        for g in (gdi, gdo, gni, gno):
            g[...] = jnp.zeros_like(g)

    def fold(x):
        return jnp.sum(x.reshape(x.shape[0] // 8, 8, x.shape[1]), 0)

    def step(t, e):
        i = steps - 1 - t
        w = e + cot[i]
        s = s_in[i]
        f = delta_time * w
        g = w * noise[i] * s * (1.0 - s)
        fb, gb = f.astype(BF), g.astype(BF)
        fb_all[i] = fb
        gb_all[i] = gb
        bias_out[0] += fold(f)
        bias_out[1] += fold(g)
        acc = w
        for c in range(CHUNKS):
            cols = slice(c * chunk, (c + 1) * chunk)
            u = u_in[i, :, cols].astype(F32)
            v = v_in[i, :, cols].astype(F32)
            p = matmul(fb, dot_[:, cols]) * (1.0 - u * u)
            r = matmul(gb, not_[:, cols]) * (1.0 - v * v)
            pb, rb = p.astype(BF), r.astype(BF)
            pb_all[i, :, cols] = pb
            rb_all[i, :, cols] = rb
            bias_hidden[0, :, cols] += fold(p)
            bias_hidden[1, :, cols] += fold(r)
            acc = acc + matmul(pb, dit[cols, :]) + matmul(rb, nit[cols, :])
        adjoints[i] = acc
        return acc

    carry[...] = lax.fori_loop(0, steps, step, carry[...])

    flat = steps * rows
    q = q_in[...].reshape(flat, L)
    fb = fb_all[...].reshape(flat, L)
    gb = gb_all[...].reshape(flat, L)
    for c in range(CHUNKS):
        cols = slice(c * chunk, (c + 1) * chunk)
        gdi[:, cols] += matmul_rows(q, pb_all[:, :, cols].reshape(flat, chunk))
        gni[:, cols] += matmul_rows(q, rb_all[:, :, cols].reshape(flat, chunk))
        gdo[cols, :] += matmul_rows(u_in[:, :, cols].reshape(flat, chunk), fb)
        gno[cols, :] += matmul_rows(v_in[:, :, cols].reshape(flat, chunk), gb)


def whole(shape):
    return pl.BlockSpec(shape, lambda g: (0,) * len(shape), pipeline_mode=pl.Buffered(1))


def forward(start, noise, params):
    total, rows, width = noise.shape
    sections = 8
    here = total // sections

    def block(cols):
        return pl.BlockSpec((here, rows, cols), lambda g: (g, 0, 0))

    return pl.pallas_call(
        forward_kernel,
        grid=(sections,),
        in_specs=[whole(start.shape), block(L)] + [whole(p.shape) for p in params],
        out_specs=[block(L), block(L), block(H), block(H), block(L)],
        out_shape=[
            jax.ShapeDtypeStruct((total, rows, L), F32),
            jax.ShapeDtypeStruct((total, rows, L), BF),
            jax.ShapeDtypeStruct((total, rows, H), BF),
            jax.ShapeDtypeStruct((total, rows, H), BF),
            jax.ShapeDtypeStruct((total, rows, L), F32),
        ],
        scratch_shapes=[pltpu.VMEM((rows, L), F32)],
        name="sde_forward",
        cost_estimate=pl.CostEstimate(flops=8_600_000_000, bytes_accessed=20_000_000, transcendentals=4_000_000),
        compiler_params=pltpu.CompilerParams(vmem_limit_bytes=24 * 1024 * 1024),
    )(start, noise, *params)


def backward(cot, noise, saved, weights):
    total, rows, width = noise.shape
    sections = 8
    here = total // sections
    last = sections - 1

    def block(cols):
        return pl.BlockSpec((here, rows, cols), lambda g: (last - g, 0, 0))

    sums = [(L, H), (H, L), (L, H), (H, L), (2, 8, H), (2, 8, L)]
    return pl.pallas_call(
        backward_kernel,
        grid=(sections,),
        in_specs=[block(L), block(L), block(L), block(H), block(H), block(L)] + [whole(p.shape) for p in weights],
        out_specs=[block(L)] + [whole(s) for s in sums],
        out_shape=[jax.ShapeDtypeStruct((total, rows, L), F32)] + [jax.ShapeDtypeStruct(s, F32) for s in sums],
        scratch_shapes=[
            pltpu.VMEM((rows, L), F32),
            pltpu.VMEM((here, rows, H), BF),
            pltpu.VMEM((here, rows, H), BF),
            pltpu.VMEM((here, rows, L), BF),
            pltpu.VMEM((here, rows, L), BF),
        ],
        name="sde_backward",
        cost_estimate=pl.CostEstimate(flops=13_000_000_000, bytes_accessed=24_000_000, transcendentals=0),
        compiler_params=pltpu.CompilerParams(vmem_limit_bytes=32 * 1024 * 1024),
    )(cot, noise, *saved, *weights)


def clip_factor(total):
    limit = 0.5 * math.sqrt(4 * L * H + 2 * H + 2 * L)
    return jnp.minimum(1.0, limit / jnp.sqrt(total))


def shards(
    initial_state, increments, cotangents,
    drift_inner, drift_hidden, drift_outer, drift_offset,
    noise_inner, noise_hidden, noise_outer, noise_offset,
):
    segments = lax.axis_size("tm")
    segment = lax.axis_index("tm")
    rows = increments.shape[1] // segments
    noise = lax.all_to_all(increments, "tm", 1, 0, tiled=True)
    cot = lax.all_to_all(cotangents, "tm", 1, 0, tiled=True)
    start = lax.dynamic_slice_in_dim(initial_state, segment * rows, rows, 0)
    states, q, u, v, s = forward(
        start,
        noise,
        (
            drift_inner, drift_hidden[None], drift_outer, drift_offset[None],
            noise_inner, noise_hidden[None], noise_outer, noise_offset[None],
        ),
    )
    adjoints, gdi, gdo, gni, gno, bias_hidden, bias_out = backward(
        cot, noise, (q, u, v, s), (drift_outer.T, drift_inner.T, noise_outer.T, noise_inner.T)
    )
    states = lax.all_to_all(states, "tm", 0, 1, tiled=True)
    adjoints = lax.all_to_all(adjoints, "tm", 0, 1, tiled=True)
    bias_hidden, bias_out = jnp.sum(bias_hidden, 1), jnp.sum(bias_out, 1)
    grads = (
        gdi, bias_hidden[0], gdo, bias_out[0],
        gni, bias_hidden[1], gno, bias_out[1],
    )
    summed = lax.psum(grads, ("tm", "batch"))
    total = sum(jnp.sum(jnp.square(entry)) for entry in summed)
    factor = clip_factor(total)
    return (states, adjoints, *(entry * factor for entry in summed))


def solution(mesh):
    split = P("tm", "batch", None)
    return jax.shard_map(
        shards,
        mesh=mesh,
        in_specs=(P("batch", None), split, split) + (P(),) * 8,
        out_specs=(split, split) + (P(),) * 8,
        check_vma=False,
    )
```

```python
import math

import jax
import jax.numpy as jnp
from jax import lax
from jax.experimental import pallas as pl
from jax.experimental.pallas import tpu as pltpu
from jax.sharding import PartitionSpec as P

L = 256
H = 1024
CHUNKS = 4
delta_time = 0.05
LANES = 128
INNER = L * H // (8 * LANES)
COLORS = 3
SIDE = 4
TILES = COLORS * SIDE**3 * 3
MESH = pl.DeviceIdType.MESH
F32 = jnp.float32
BF = jnp.bfloat16


def matmul(left, right):
    return jnp.dot(left, right, preferred_element_type=F32)


def matmul_rows(left, right):
    return lax.dot_general(left, right, (((0,), (0,)), ((), ())), preferred_element_type=F32)


def forward_kernel(start, noise, di, dh, do, dof, ni, nh, no, nof, states, q_out, u_out, v_out, s_out, carry):
    steps, rows, width = noise.shape
    chunk = H // CHUNKS

    @pl.when(pl.program_id(0) == 0)
    def _():
        carry[...] = start[...]

    def step(i, z):
        q = z.astype(BF)
        q_out[i] = q
        drift = noisy = None
        for c in range(CHUNKS):
            cols = slice(c * chunk, (c + 1) * chunk)
            u = jnp.tanh(matmul(q, di[:, cols]) + dh[:, cols]).astype(BF)
            v = jnp.tanh(matmul(q, ni[:, cols]) + nh[:, cols]).astype(BF)
            u_out[i, :, cols] = u
            v_out[i, :, cols] = v
            a, b = matmul(u, do[cols, :]), matmul(v, no[cols, :])
            drift = a if drift is None else drift + a
            noisy = b if noisy is None else noisy + b
        s = jax.nn.sigmoid(noisy + nof[...])
        s_out[i] = s
        z = z + delta_time * (drift + dof[...]) + s * noise[i]
        states[i] = z
        return z

    carry[...] = lax.fori_loop(0, steps, step, carry[...])


def backward_kernel(
    cot, noise, q_in, u_in, v_in, s_in, dot_, dit, not_, nit,
    adjoints, grads,
    carry, pb_all, rb_all, fb_all, gb_all, bias_hidden, bias_out,
):
    steps, rows, width = noise.shape
    chunk = H // CHUNKS
    first = pl.program_id(0) == 0

    @pl.when(first)
    def _():
        carry[...] = jnp.zeros_like(carry)
        bias_hidden[...] = jnp.zeros_like(bias_hidden)
        bias_out[...] = jnp.zeros_like(bias_out)
        grads[...] = jnp.zeros_like(grads)

    def fold(x):
        return jnp.sum(x.reshape(x.shape[0] // 8, 8, x.shape[1]), 0)

    def step(t, e):
        i = steps - 1 - t
        w = e + cot[i]
        s = s_in[i]
        f = delta_time * w
        g = w * noise[i] * s * (1.0 - s)
        fb, gb = f.astype(BF), g.astype(BF)
        fb_all[i] = fb
        gb_all[i] = gb
        bias_out[0] += fold(f)
        bias_out[1] += fold(g)
        acc = w
        for c in range(CHUNKS):
            cols = slice(c * chunk, (c + 1) * chunk)
            u = u_in[i, :, cols].astype(F32)
            v = v_in[i, :, cols].astype(F32)
            p = matmul(fb, dot_[:, cols]) * (1.0 - u * u)
            r = matmul(gb, not_[:, cols]) * (1.0 - v * v)
            pb, rb = p.astype(BF), r.astype(BF)
            pb_all[i, :, cols] = pb
            rb_all[i, :, cols] = rb
            bias_hidden[0, :, cols] += fold(p)
            bias_hidden[1, :, cols] += fold(r)
            acc = acc + matmul(pb, dit[cols, :]) + matmul(rb, nit[cols, :])
        adjoints[i] = acc
        return acc

    carry[...] = lax.fori_loop(0, steps, step, carry[...])

    flat = steps * rows
    q = q_in[...].reshape(flat, L)
    fb = fb_all[...].reshape(flat, L)
    gb = gb_all[...].reshape(flat, L)

    def add(net, base, stride, value):
        for h in range(2):
            part = value[:, h * LANES : (h + 1) * LANES].reshape(chunk // 8, 8, LANES)
            at = pl.ds(base + h, chunk // 8, stride=stride)
            grads[net, at] = grads[net, at] + part

    for c in range(CHUNKS):
        cols = slice(c * chunk, (c + 1) * chunk)
        add(0, 2 * c, H // LANES, matmul_rows(q, pb_all[:, :, cols].reshape(flat, chunk)))
        add(1, 2 * c, H // LANES, matmul_rows(q, rb_all[:, :, cols].reshape(flat, chunk)))
        add(0, INNER + c * chunk // 4, L // LANES, matmul_rows(u_in[:, :, cols].reshape(flat, chunk), fb))
        add(1, INNER + c * chunk // 4, L // LANES, matmul_rows(v_in[:, :, cols].reshape(flat, chunk), gb))

    @pl.when(pl.program_id(0) == pl.num_programs(0) - 1)
    def _():
        for net in range(2):
            hidden = jnp.sum(bias_hidden[net], 0, keepdims=True)
            out = jnp.sum(bias_out[net], 0, keepdims=True)
            for j in range(H // LANES):
                grads[net, 2 * INNER, j : j + 1, :] = hidden[:, j * LANES : (j + 1) * LANES]
            for j in range(L // LANES):
                grads[net, 2 * INNER + 1, j : j + 1, :] = out[:, j * LANES : (j + 1) * LANES]


def whole(shape):
    return pl.BlockSpec(shape, lambda g: (0,) * len(shape), pipeline_mode=pl.Buffered(1))


def forward(start, noise, params):
    total, rows, width = noise.shape
    sections = 8
    here = total // sections

    def block(cols):
        return pl.BlockSpec((here, rows, cols), lambda g: (g, 0, 0))

    return pl.pallas_call(
        forward_kernel,
        grid=(sections,),
        in_specs=[whole(start.shape), block(L)] + [whole(p.shape) for p in params],
        out_specs=[block(L), block(L), block(H), block(H), block(L)],
        out_shape=[
            jax.ShapeDtypeStruct((total, rows, L), F32),
            jax.ShapeDtypeStruct((total, rows, L), BF),
            jax.ShapeDtypeStruct((total, rows, H), BF),
            jax.ShapeDtypeStruct((total, rows, H), BF),
            jax.ShapeDtypeStruct((total, rows, L), F32),
        ],
        scratch_shapes=[pltpu.VMEM((rows, L), F32)],
        name="sde_forward",
        cost_estimate=pl.CostEstimate(flops=8_600_000_000, bytes_accessed=20_000_000, transcendentals=4_000_000),
    )(start, noise, *params)


def backward(cot, noise, saved, weights):
    total, rows, width = noise.shape
    sections = 8
    here = total // sections
    last = sections - 1

    def block(cols):
        return pl.BlockSpec((here, rows, cols), lambda g: (last - g, 0, 0))

    sums = (2, TILES, 8, LANES)
    return pl.pallas_call(
        backward_kernel,
        grid=(sections,),
        in_specs=[block(L), block(L), block(L), block(H), block(H), block(L)] + [whole(p.shape) for p in weights],
        out_specs=[block(L), whole(sums)],
        out_shape=[jax.ShapeDtypeStruct((total, rows, L), F32), jax.ShapeDtypeStruct(sums, F32)],
        scratch_shapes=[
            pltpu.VMEM((rows, L), F32),
            pltpu.VMEM((here, rows, H), BF),
            pltpu.VMEM((here, rows, H), BF),
            pltpu.VMEM((here, rows, L), BF),
            pltpu.VMEM((here, rows, L), BF),
            pltpu.VMEM((2, 8, H), F32),
            pltpu.VMEM((2, 8, L), F32),
        ],
        name="sde_backward",
        cost_estimate=pl.CostEstimate(flops=13_000_000_000, bytes_accessed=24_000_000, transcendentals=0),
    )(cot, noise, *saved, *weights)


def reduce_kernel(mine, out, square, held, landed1, landed2, landed3, sib_send, sib_recv, send, recv, back_send, back_recv):
    tm = lax.axis_index("tm")
    batch = lax.axis_index("batch")
    core = lax.rem(tm, 2)
    place = (lax.div(tm, 2), lax.div(batch, SIDE), lax.rem(batch, SIDE))
    other = 1 - core
    sibling = (tm + 1 - 2 * core, batch)

    def partner(axis, distance):
        moved = lax.rem(place[axis] + distance, SIDE)
        x, y, z = (moved if a == axis else place[a] for a in range(3))
        return (2 * x + core, SIDE * y + z)

    barrier = pltpu.get_barrier_semaphore()
    pl.semaphore_signal(barrier, inc=1, device_id=sibling, device_id_type=MESH)
    for axis in range(3):
        for distance in range(1, SIDE):
            pl.semaphore_signal(barrier, inc=1, device_id=partner(axis, distance), device_id_type=MESH)
    pl.semaphore_wait(barrier, 10)

    size = TILES // COLORS
    orders = [tuple((color + phase) % 3 for phase in range(3)) for color in range(COLORS)]
    landed = (landed1, landed2, landed3)
    sizes = [size // SIDE ** (phase + 1) for phase in range(3)]

    def remote(src, dst, send_sem, recv_sem, device):
        copy = pltpu.make_async_remote_copy(
            src_ref=src, dst_ref=dst, send_sem=send_sem, recv_sem=recv_sem, device_id=device, device_id_type=MESH
        )
        copy.start()
        return copy

    swaps = []
    for color in range(COLORS):
        span = pl.ds(color * size, size)
        swaps.append(
            remote(mine.at[other, span], held.at[span], sib_send.at[color], sib_recv.at[color], sibling)
        )
    sent = []
    bases = [color * size for color in range(COLORS)]
    for phase in range(3):
        moves = []
        for color in range(COLORS):
            axis, part = orders[color][phase], sizes[phase]
            if phase == 0:
                swaps[color].wait_recv()
                span = pl.ds(color * size, size)
                held[span] = held[span] + mine[core, span]
            else:
                for move in sent[color]:
                    move.wait_recv()
                span = pl.ds(bases[color], part * SIDE)
                got = landed[phase - 1]
                held[span] = held[span] + got[color, 0] + (got[color, 1] + got[color, 2])
            row = []
            for distance in range(1, SIDE):
                to = lax.rem(place[axis] + distance, SIDE)
                row.append(
                    remote(
                        held.at[pl.ds(bases[color] + to * part, part)],
                        landed[phase].at[color, distance - 1],
                        send.at[color, phase, distance - 1],
                        recv.at[color, phase, distance - 1],
                        partner(axis, distance),
                    )
                )
            moves.append(row)
            bases[color] = bases[color] + place[axis] * part
        sent = moves
        if phase == 0:
            first = moves
        elif phase == 1:
            second = moves
    third = sent
    gathers = []
    for color in range(COLORS):
        for move in third[color]:
            move.wait_recv()
        span = pl.ds(bases[color], sizes[2])
        out[core, span] = held[span] + landed3[color, 0] + (landed3[color, 1] + landed3[color, 2])
    moves = [None] * COLORS
    for phase in (2, 1, 0):
        part = sizes[phase]
        for color in range(COLORS):
            axis = orders[color][phase]
            if phase < 2:
                for move in moves[color]:
                    move.wait_recv()
            span = pl.ds(bases[color], part)
            row = [
                remote(
                    out.at[core, span],
                    out.at[core, span],
                    send.at[color, 5 - phase, distance - 1],
                    recv.at[color, 5 - phase, distance - 1],
                    partner(axis, distance),
                )
                for distance in range(1, SIDE)
            ]
            gathers.extend(row)
            if phase == 0:
                gathers.append(
                    remote(out.at[core, span], out.at[core, span], back_send.at[color, 0], back_recv.at[color, 0], sibling)
                )
            moves[color] = row
            bases[color] = bases[color] - place[axis] * part
    backs = []
    for color in range(COLORS):
        axis = orders[color][0]
        part = sizes[0]
        for distance in range(1, SIDE):
            moves[color][distance - 1].wait_recv()
            source = lax.rem(place[axis] + SIDE - distance, SIDE)
            span = pl.ds(bases[color] + source * part, part)
            backs.append(
                remote(
                    out.at[core, span], out.at[core, span],
                    back_send.at[color, distance], back_recv.at[color, distance], sibling,
                )
            )
    for color in range(COLORS):
        axis = orders[color][0]
        for distance in range(SIDE):
            source = lax.rem(place[axis] + SIDE - distance, SIDE)
            view = out.at[other, pl.ds(color * size + source * sizes[0], sizes[0])]
            pltpu.make_async_copy(view, view, back_recv.at[color, distance]).wait()
    total = jnp.zeros((8, LANES), F32)
    step = 64

    def squares(i, total):
        a, b = out[0, pl.ds(i * step, step)], out[1, pl.ds(i * step, step)]
        return total + jnp.sum(a * a + b * b, 0)

    square[...] = lax.fori_loop(0, TILES // step, squares, total)
    for move in swaps + backs:
        move.wait_send()
    for rows in (first, second, third):
        for row in rows:
            for move in row:
                move.wait_send()
    for move in gathers:
        move.wait_send()


def all_reduce(grads):
    dma = pltpu.SemaphoreType.DMA
    size = TILES // COLORS
    return pl.pallas_call(
        reduce_kernel,
        in_specs=[pl.BlockSpec(memory_space=pltpu.VMEM)],
        out_specs=[pl.BlockSpec(memory_space=pltpu.VMEM)] * 2,
        out_shape=[jax.ShapeDtypeStruct(grads.shape, F32), jax.ShapeDtypeStruct((8, LANES), F32)],
        scratch_shapes=[
            pltpu.VMEM((TILES, 8, LANES), F32),
            *(pltpu.VMEM((COLORS, 3, size // SIDE ** (p + 1), 8, LANES), F32) for p in range(3)),
            dma((COLORS,)), dma((COLORS,)),
            dma((COLORS, 6, 3)), dma((COLORS, 6, 3)),
            dma((COLORS, 4)), dma((COLORS, 4)),
        ],
        name="sde_reduce",
        compiler_params=pltpu.CompilerParams(collective_id=0, has_side_effects=True),
    )(grads)


def clip_factor(total):
    limit = 0.5 * math.sqrt(4 * L * H + 2 * H + 2 * L)
    return jnp.minimum(1.0, limit / jnp.sqrt(total))


def shards(
    initial_state, increments, cotangents,
    drift_inner, drift_hidden, drift_outer, drift_offset,
    noise_inner, noise_hidden, noise_outer, noise_offset,
):
    segments = lax.axis_size("tm")
    segment = lax.axis_index("tm")
    rows = increments.shape[1] // segments
    noise = lax.all_to_all(increments, "tm", 1, 0, tiled=True)
    cot = lax.all_to_all(cotangents, "tm", 1, 0, tiled=True)
    start = lax.dynamic_slice_in_dim(initial_state, segment * rows, rows, 0)
    states, q, u, v, s = forward(
        start,
        noise,
        (
            drift_inner, drift_hidden[None], drift_outer, drift_offset[None],
            noise_inner, noise_hidden[None], noise_outer, noise_offset[None],
        ),
    )
    adjoints, grads = backward(
        cot, noise, (q, u, v, s), (drift_outer.T, drift_inner.T, noise_outer.T, noise_inner.T)
    )
    states = lax.all_to_all(states, "tm", 0, 1, tiled=True)
    adjoints = lax.all_to_all(adjoints, "tm", 0, 1, tiled=True)
    summed, square = all_reduce(grads)
    factor = clip_factor(jnp.sum(square))

    def matrix(net, base, rows, columns):
        tiles = summed[net, base : base + INNER].reshape(rows // 8, columns // LANES, 8, LANES)
        return tiles.transpose(0, 2, 1, 3).reshape(rows, columns) * factor

    result = []
    for net in range(2):
        result += [
            matrix(net, 0, L, H),
            summed[net, 2 * INNER].reshape(H) * factor,
            matrix(net, INNER, H, L),
            summed[net, 2 * INNER + 1, : L // LANES].reshape(L) * factor,
        ]
    return (states, adjoints, *result)


def solution(mesh):
    split = P("tm", "batch", None)
    return jax.shard_map(
        shards,
        mesh=mesh,
        in_specs=(P("batch", None), split, split) + (P(),) * 8,
        out_specs=(split, split) + (P(),) * 8,
        check_vma=False,
    )
```

```python
import math

import jax
import jax.numpy as jnp
from jax import lax
from jax.experimental import pallas as pl
from jax.experimental.pallas import tpu as pltpu
from jax.sharding import PartitionSpec as P

L = 256
H = 1024
CHUNKS = 4
SECTIONS = 8
SENDER = (0, 0, 0, 1, 2, 3, 4, 5)
COT_AT = (4, 3, 6, 5, 7, 6, 3, 2)
delta_time = 0.05
LANES = 128
INNER = L * H // (8 * LANES)
COLORS = 3
SIDE = 4
TILES = COLORS * SIDE**3 * 3
MESH = pl.DeviceIdType.MESH
F32 = jnp.float32
BF = jnp.bfloat16


def matmul(left, right):
    return jnp.dot(left, right, preferred_element_type=F32)


def matmul_rows(left, right):
    return lax.dot_general(left, right, (((0,), (0,)), ((), ())), preferred_element_type=F32)


def window_kernel(
    start, noise_hbm, cot_hbm, di, dh, do, dof, ni, nh, no, nof,
    states_hbm, adjoints_hbm, out, square,
    noise, cot, states, adjoints, q_all, u_all, v_all, s_all,
    pb_all, rb_all, fb_all, gb_all, bias_hidden, bias_out, begin,
    dot_, dit, not_, nit, grads, held, landed1, landed2, landed3,
    own, noise_send, noise_recv, cot_send, cot_recv, states_send, states_recv, adj_send, adj_recv,
    sib_send, sib_recv, send, recv, back_send, back_recv,
):
    tm = lax.axis_index("tm")
    batch = lax.axis_index("batch")
    core = lax.rem(tm, 2)
    place = (lax.div(tm, 2), lax.div(batch, SIDE), lax.rem(batch, SIDE))
    other = 1 - core
    sibling = (tm + 1 - 2 * core, batch)
    here = noise_hbm.shape[0]
    rows = noise_hbm.shape[1] // SECTIONS
    total_steps = here * SECTIONS
    chunk = H // CHUNKS

    def partner(axis, distance):
        moved = lax.rem(place[axis] + distance, SIDE)
        x, y, z = (moved if a == axis else place[a] for a in range(3))
        return (2 * x + core, SIDE * y + z)

    def pick(table):
        chosen = jnp.int32(table[0])
        for index in range(1, len(table)):
            chosen = jnp.where(tm == index, table[index], chosen)
        return chosen

    def strip(index):
        return pl.ds(pl.multiple_of(index * rows, rows), rows)

    def remote(src, dst, send_sem, recv_sem, device):
        copy = pltpu.make_async_remote_copy(
            src_ref=src, dst_ref=dst, send_sem=send_sem, recv_sem=recv_sem, device_id=device, device_id_type=MESH
        )
        copy.start()
        return copy

    def local(src, dst, sem):
        copy = pltpu.make_async_copy(src, dst, sem)
        copy.start()
        return copy

    def wait_bytes(view, sem):
        pltpu.make_async_copy(view, view, sem).wait()

    begin_copy = local(start.at[strip(tm)], begin, own.at[0])

    def own_noise(m, _):
        local(noise_hbm.at[m, strip(tm)], noise.at[tm * here + m], noise_recv.at[tm * here + m])
        return 0

    lax.fori_loop(0, here, own_noise, 0)
    mine = pl.ds(tm * here, here)
    local(cot_hbm.at[:, strip(tm)], cot.at[mine], cot_recv.at[tm])

    barrier = pltpu.get_barrier_semaphore()
    for distance in range(1, SECTIONS):
        pl.semaphore_signal(
            barrier, inc=1, device_id=(lax.rem(tm + distance, SECTIONS), batch), device_id_type=MESH
        )
    for axis in (1, 2):
        for distance in range(1, SIDE):
            pl.semaphore_signal(barrier, inc=1, device_id=partner(axis, distance), device_id_type=MESH)
    pl.semaphore_wait(barrier, 13)

    def send_noise(m):
        for distance in range(1, SECTIONS):
            to = lax.rem(tm + distance, SECTIONS)
            k = tm * here + m
            remote(noise_hbm.at[m, strip(to)], noise.at[k], noise_send, noise_recv.at[k], (to, batch))

    def send_cot():
        for distance in range(1, SECTIONS):
            to = lax.rem(tm + distance, SECTIONS)
            remote(cot_hbm.at[:, strip(to)], cot.at[mine], cot_send, cot_recv.at[tm], (to, batch))

    @pl.when(tm == 0)
    def _():
        def each(m, _):
            send_noise(m)
            return 0

        lax.fori_loop(0, here, each, 0)

    dot_[...] = do[...].T
    not_[...] = no[...].T
    dit[...] = di[...].T
    nit[...] = ni[...].T
    grads[...] = jnp.zeros_like(grads)
    bias_hidden[...] = jnp.zeros_like(bias_hidden)
    bias_out[...] = jnp.zeros_like(bias_out)
    noise_at = pick(SENDER)
    cot_at = pick(COT_AT)
    begin_copy.wait()

    def forward_section(g, z):
        @pl.when(g == cot_at)
        def _():
            send_cot()

        paced = (g == noise_at) & (tm != 0)

        def step(m, z):
            k = g * here + m

            @pl.when(paced)
            def _():
                send_noise(m)

            q = z.astype(BF)
            q_all[k] = q
            u = jnp.tanh(matmul(q, di[...]) + dh[...]).astype(BF)
            v = jnp.tanh(matmul(q, ni[...]) + nh[...]).astype(BF)
            u_all[k] = u
            v_all[k] = v
            drift = matmul(u, do[...])
            s = jax.nn.sigmoid(matmul(v, no[...]) + nof[...])
            s_all[k] = s
            wait_bytes(noise.at[k], noise_recv.at[k])
            z = z + delta_time * (drift + dof[...]) + s * noise[k]
            states[k] = z
            return z

        return lax.fori_loop(0, here, step, z)

    lax.fori_loop(0, SECTIONS, forward_section, begin[...])

    local(states.at[mine], states_hbm.at[:, strip(tm)], own.at[1])

    def fold(x):
        return jnp.sum(x.reshape(x.shape[0] // 8, 8, x.shape[1]), 0)

    def add(net, base, stride, value):
        for h in range(2):
            part = value[:, h * LANES : (h + 1) * LANES].reshape(chunk // 8, 8, LANES)
            at = pl.ds(base + h, chunk // 8, stride=stride)
            grads[net, at] = grads[net, at] + part

    def backward_section(t, e):
        g = SECTIONS - 1 - t
        section = pl.ds(g * here, here)

        @pl.when(t < SECTIONS - 1)
        def _():
            to = lax.rem(tm + 1 + t, SECTIONS)
            remote(
                states.at[pl.ds(to * here, here)], states_hbm.at[:, strip(tm)], states_send, states_recv, (to, batch)
            )

        wait_bytes(cot.at[section], cot_recv.at[g])

        def step(back, e):
            m = here - 1 - back
            k = g * here + m
            w = e + cot[k]
            s = s_all[k]
            f = delta_time * w
            r0 = w * noise[k] * s * (1.0 - s)
            fb, gb = f.astype(BF), r0.astype(BF)
            fb_all[m] = fb
            gb_all[m] = gb
            bias_out[0] += fold(f)
            bias_out[1] += fold(r0)
            acc = w
            for c in range(CHUNKS):
                cols = slice(c * chunk, (c + 1) * chunk)
                u = u_all[k, :, cols].astype(F32)
                v = v_all[k, :, cols].astype(F32)
                p = matmul(fb, dot_[:, cols]) * (1.0 - u * u)
                r = matmul(gb, not_[:, cols]) * (1.0 - v * v)
                pb, rb = p.astype(BF), r.astype(BF)
                pb_all[m, :, cols] = pb
                rb_all[m, :, cols] = rb
                bias_hidden[0, :, cols] += fold(p)
                bias_hidden[1, :, cols] += fold(r)
                acc = acc + matmul(pb, dit[cols, :]) + matmul(rb, nit[cols, :])
            adjoints[k] = acc
            return acc

        e = lax.fori_loop(0, here, step, e)

        flat = here * rows
        q = q_all[section].reshape(flat, L)
        fb = fb_all[...].reshape(flat, L)
        gb = gb_all[...].reshape(flat, L)
        for c in range(CHUNKS):
            cols = slice(c * chunk, (c + 1) * chunk)
            add(0, 2 * c, H // LANES, matmul_rows(q, pb_all[:, :, cols].reshape(flat, chunk)))
            add(1, 2 * c, H // LANES, matmul_rows(q, rb_all[:, :, cols].reshape(flat, chunk)))
            add(0, INNER + c * chunk // 4, L // LANES, matmul_rows(u_all[section, :, cols].reshape(flat, chunk), fb))
            add(1, INNER + c * chunk // 4, L // LANES, matmul_rows(v_all[section, :, cols].reshape(flat, chunk), gb))

        @pl.when(g == tm)
        def _():
            local(adjoints.at[mine], adjoints_hbm.at[:, strip(tm)], own.at[2])

        @pl.when(g != tm)
        def _():
            remote(adjoints.at[section], adjoints_hbm.at[:, strip(tm)], adj_send, adj_recv, (g, batch))

        return e

    lax.fori_loop(0, SECTIONS, backward_section, jnp.zeros((rows, L), F32))

    for net in range(2):
        hidden = jnp.sum(bias_hidden[net], 0, keepdims=True)
        last = jnp.sum(bias_out[net], 0, keepdims=True)
        for j in range(H // LANES):
            grads[net, 2 * INNER, j : j + 1, :] = hidden[:, j * LANES : (j + 1) * LANES]
        for j in range(L // LANES):
            grads[net, 2 * INNER + 1, j : j + 1, :] = last[:, j * LANES : (j + 1) * LANES]

    size = TILES // COLORS
    orders = [tuple((color + phase) % 3 for phase in range(3)) for color in range(COLORS)]
    landed = (landed1, landed2, landed3)
    sizes = [size // SIDE ** (phase + 1) for phase in range(3)]

    swaps = []
    for color in range(COLORS):
        span = pl.ds(color * size, size)
        swaps.append(
            remote(grads.at[other, span], held.at[span], sib_send.at[color], sib_recv.at[color], sibling)
        )
    sent = []
    bases = [color * size for color in range(COLORS)]
    for phase in range(3):
        moves = []
        for color in range(COLORS):
            axis, part = orders[color][phase], sizes[phase]
            if phase == 0:
                swaps[color].wait_recv()
                span = pl.ds(color * size, size)
                held[span] = held[span] + grads[core, span]
            else:
                for move in sent[color]:
                    move.wait_recv()
                span = pl.ds(bases[color], part * SIDE)
                got = landed[phase - 1]
                held[span] = held[span] + got[color, 0] + (got[color, 1] + got[color, 2])
            row = []
            for distance in range(1, SIDE):
                to = lax.rem(place[axis] + distance, SIDE)
                row.append(
                    remote(
                        held.at[pl.ds(bases[color] + to * part, part)],
                        landed[phase].at[color, distance - 1],
                        send.at[color, phase, distance - 1],
                        recv.at[color, phase, distance - 1],
                        partner(axis, distance),
                    )
                )
            moves.append(row)
            bases[color] = bases[color] + place[axis] * part
        sent = moves
        if phase == 0:
            first = moves
        elif phase == 1:
            second = moves
    third = sent
    gathers = []
    for color in range(COLORS):
        for move in third[color]:
            move.wait_recv()
        span = pl.ds(bases[color], sizes[2])
        out[core, span] = held[span] + landed3[color, 0] + (landed3[color, 1] + landed3[color, 2])
    moves = [None] * COLORS
    for phase in (2, 1, 0):
        part = sizes[phase]
        for color in range(COLORS):
            axis = orders[color][phase]
            if phase < 2:
                for move in moves[color]:
                    move.wait_recv()
            span = pl.ds(bases[color], part)
            row = [
                remote(
                    out.at[core, span],
                    out.at[core, span],
                    send.at[color, 5 - phase, distance - 1],
                    recv.at[color, 5 - phase, distance - 1],
                    partner(axis, distance),
                )
                for distance in range(1, SIDE)
            ]
            gathers.extend(row)
            if phase == 0:
                gathers.append(
                    remote(out.at[core, span], out.at[core, span], back_send.at[color, 0], back_recv.at[color, 0], sibling)
                )
            moves[color] = row
            bases[color] = bases[color] - place[axis] * part
    backs = []
    for color in range(COLORS):
        axis = orders[color][0]
        part = sizes[0]
        for distance in range(1, SIDE):
            moves[color][distance - 1].wait_recv()
            source = lax.rem(place[axis] + SIDE - distance, SIDE)
            span = pl.ds(bases[color] + source * part, part)
            backs.append(
                remote(
                    out.at[core, span], out.at[core, span],
                    back_send.at[color, distance], back_recv.at[color, distance], sibling,
                )
            )
    for color in range(COLORS):
        axis = orders[color][0]
        for distance in range(SIDE):
            source = lax.rem(place[axis] + SIDE - distance, SIDE)
            view = out.at[other, pl.ds(color * size + source * sizes[0], sizes[0])]
            pltpu.make_async_copy(view, view, back_recv.at[color, distance]).wait()
    total = jnp.zeros((8, LANES), F32)
    step = 64

    def squares(i, total):
        a, b = out[0, pl.ds(i * step, step)], out[1, pl.ds(i * step, step)]
        return total + jnp.sum(a * a + b * b, 0)

    square[...] = lax.fori_loop(0, TILES // step, squares, total)
    for move in swaps + backs:
        move.wait_send()
    for group in (first, second, third):
        for row in group:
            for move in row:
                move.wait_send()
    for move in gathers:
        move.wait_send()
    others = pl.ds(0, total_steps - here)
    for sem in (noise_send, cot_send, states_send, adj_send):
        wait_bytes(noise.at[others], sem)
    sent_rows = pl.ds(0, rows * (SECTIONS - 1))
    wait_bytes(states_hbm.at[:, sent_rows], states_recv)
    wait_bytes(adjoints_hbm.at[:, sent_rows], adj_recv)
    wait_bytes(states.at[mine], own.at[1])
    wait_bytes(states.at[mine], own.at[2])


def window(start, noise, cot, params):
    dma = pltpu.SemaphoreType.DMA
    size = TILES // COLORS
    here, wide, _ = noise.shape
    steps, rows = here * SECTIONS, wide // SECTIONS
    vmem = pl.BlockSpec(memory_space=pltpu.VMEM)
    anywhere = pl.BlockSpec(memory_space=pl.ANY)
    V = pltpu.VMEM
    sums = (2, TILES, 8, LANES)
    return pl.pallas_call(
        window_kernel,
        in_specs=[anywhere] * 3 + [vmem] * 8,
        out_specs=[anywhere] * 2 + [vmem] * 2,
        out_shape=[
            jax.ShapeDtypeStruct(noise.shape, F32),
            jax.ShapeDtypeStruct(noise.shape, F32),
            jax.ShapeDtypeStruct(sums, F32),
            jax.ShapeDtypeStruct((8, LANES), F32),
        ],
        scratch_shapes=[
            *(V((steps, rows, L), F32) for _ in range(4)),
            V((steps, rows, L), BF), V((steps, rows, H), BF), V((steps, rows, H), BF), V((steps, rows, L), F32),
            V((here, rows, H), BF), V((here, rows, H), BF), V((here, rows, L), BF), V((here, rows, L), BF),
            V((2, 8, H), F32), V((2, 8, L), F32), V((rows, L), F32),
            V((L, H), BF), V((H, L), BF), V((L, H), BF), V((H, L), BF),
            V(sums, F32),
            V((TILES, 8, LANES), F32),
            *(V((COLORS, 3, size // SIDE ** (p + 1), 8, LANES), F32) for p in range(3)),
            dma((3,)), dma, dma((steps,)), dma, dma((SECTIONS,)), dma, dma, dma, dma,
            dma((COLORS,)), dma((COLORS,)),
            dma((COLORS, 6, 3)), dma((COLORS, 6, 3)),
            dma((COLORS, 4)), dma((COLORS, 4)),
        ],
        name="sde_window",
        compiler_params=pltpu.CompilerParams(
            collective_id=0, has_side_effects=True, vmem_limit_bytes=62 * 1024 * 1024
        ),
    )(start, noise, cot, *params)


def clip_factor(total):
    limit = 0.5 * math.sqrt(4 * L * H + 2 * H + 2 * L)
    return jnp.minimum(1.0, limit / jnp.sqrt(total))


def shards(
    initial_state, increments, cotangents,
    drift_inner, drift_hidden, drift_outer, drift_offset,
    noise_inner, noise_hidden, noise_outer, noise_offset,
):
    states, adjoints, summed, square = window(
        initial_state,
        increments,
        cotangents,
        (
            drift_inner, drift_hidden[None], drift_outer, drift_offset[None],
            noise_inner, noise_hidden[None], noise_outer, noise_offset[None],
        ),
    )
    factor = clip_factor(jnp.sum(square))

    def matrix(net, base, rows, columns):
        tiles = summed[net, base : base + INNER].reshape(rows // 8, columns // LANES, 8, LANES)
        return tiles.transpose(0, 2, 1, 3).reshape(rows, columns) * factor

    result = []
    for net in range(2):
        result += [
            matrix(net, 0, L, H),
            summed[net, 2 * INNER].reshape(H) * factor,
            matrix(net, INNER, H, L),
            summed[net, 2 * INNER + 1, : L // LANES].reshape(L) * factor,
        ]
    return (states, adjoints, *result)


def solution(mesh):
    split = P("tm", "batch", None)
    return jax.shard_map(
        shards,
        mesh=mesh,
        in_specs=(P("batch", None), split, split) + (P(),) * 8,
        out_specs=(split, split) + (P(),) * 8,
        check_vma=False,
    )
```

```python
import math

import jax
import jax.numpy as jnp
from jax import lax
from jax.experimental import pallas as pl
from jax.experimental.pallas import tpu as pltpu
from jax.sharding import PartitionSpec as P

L = 256
H = 1024
CHUNKS = 4
SECTIONS = 8
NOISE_AT = (-1, 5, 3, 8, -1, 2, 8, 16)
COT_AT = (16, 24, 40, 32, 24, 16, -1, -1)
FINE = 2
delta_time = 0.05
LANES = 128
INNER = L * H // (8 * LANES)
COLORS = 5
SIZES = (128, 128, 128, 128, 64)
STARTS = (0, 128, 256, 384, 512)
ORDERS = ((1, 2, 0), (2, 1, 0), (1, 2, 0), (2, 1, 0), (1, 2, 0))
EARLY, LATE = (4, 0, 1), (2, 3)
SIDE = 4
TILES = sum(SIZES)
MESH = pl.DeviceIdType.MESH
F32 = jnp.float32
BF = jnp.bfloat16


def matmul(left, right):
    return jnp.dot(left, right, preferred_element_type=F32)


def matmul_rows(left, right):
    return lax.dot_general(left, right, (((0,), (0,)), ((), ())), preferred_element_type=F32)


def window_kernel(
    start, noise_hbm, cot_hbm, di, dh, do, dof, ni, nh, no, nof,
    states_hbm, adjoints_hbm, out, factor,
    noise, cot, states, adjoints, q_all, u_all, v_all, s_all,
    pb_all, rb_all, fb_all, gb_all, bias_hidden, bias_out, begin,
    dot_, dit, not_, nit, grads, held, landed1, landed2, landed3,
    own, noise_send, noise_recv, fine_recv, cot_send, cot_recv, states_send, states_recv, adj_send, adj_recv,
    sib_send, sib_recv, send, recv, back_send, back_recv,
):
    tm = lax.axis_index("tm")
    batch = lax.axis_index("batch")
    core = lax.rem(tm, 2)
    place = (lax.div(tm, 2), lax.div(batch, SIDE), lax.rem(batch, SIDE))
    other = 1 - core
    sibling = (tm + 1 - 2 * core, batch)
    here = noise_hbm.shape[0]
    rows = noise_hbm.shape[1] // SECTIONS
    total_steps = here * SECTIONS
    chunk = H // CHUNKS

    def partner(axis, distance):
        moved = lax.rem(place[axis] + distance, SIDE)
        x, y, z = (moved if a == axis else place[a] for a in range(3))
        return (2 * x + core, SIDE * y + z)

    def pick(table):
        chosen = jnp.int32(table[0])
        for index in range(1, len(table)):
            chosen = jnp.where(tm == index, table[index], chosen)
        return chosen

    def strip(index):
        return pl.ds(pl.multiple_of(index * rows, rows), rows)

    def remote(src, dst, send_sem, recv_sem, device):
        copy = pltpu.make_async_remote_copy(
            src_ref=src, dst_ref=dst, send_sem=send_sem, recv_sem=recv_sem, device_id=device, device_id_type=MESH
        )
        copy.start()
        return copy

    def local(src, dst, sem):
        copy = pltpu.make_async_copy(src, dst, sem)
        copy.start()
        return copy

    def wait_bytes(view, sem):
        pltpu.make_async_copy(view, view, sem).wait()

    begin_copy = local(start.at[strip(tm)], begin, own.at[0])

    mine = pl.ds(tm * here, here)

    @pl.when(tm < FINE)
    def _():
        def own_noise(m, _):
            k = tm * here + m
            local(noise_hbm.at[m, strip(tm)], noise.at[k], fine_recv.at[k])
            return 0

        lax.fori_loop(0, here, own_noise, 0)

    @pl.when(tm >= FINE)
    def _():
        local(noise_hbm.at[:, strip(tm)], noise.at[mine], noise_recv.at[tm])

    local(cot_hbm.at[:, strip(tm)], cot.at[mine], cot_recv.at[tm])

    barrier = pltpu.get_barrier_semaphore()
    for distance in range(1, SECTIONS):
        pl.semaphore_signal(
            barrier, inc=1, device_id=(lax.rem(tm + distance, SECTIONS), batch), device_id_type=MESH
        )
    for axis in (1, 2):
        for distance in range(1, SIDE):
            pl.semaphore_signal(barrier, inc=1, device_id=partner(axis, distance), device_id_type=MESH)
    pl.semaphore_wait(barrier, 13)

    def send_noise():
        @pl.when(tm < FINE)
        def _():
            def each(m, _):
                k = tm * here + m
                for distance in range(1, SECTIONS):
                    to = lax.rem(tm + distance, SECTIONS)
                    remote(noise_hbm.at[m, strip(to)], noise.at[k], noise_send, fine_recv.at[k], (to, batch))
                return 0

            lax.fori_loop(0, here, each, 0)

        @pl.when(tm >= FINE)
        def _():
            for distance in range(1, SECTIONS):
                to = lax.rem(tm + distance, SECTIONS)
                remote(noise_hbm.at[:, strip(to)], noise.at[mine], noise_send, noise_recv.at[tm], (to, batch))

    def send_cot():
        for distance in range(1, SECTIONS):
            to = lax.rem(tm + distance, SECTIONS)
            remote(cot_hbm.at[:, strip(to)], cot.at[mine], cot_send, cot_recv.at[tm], (to, batch))

    noise_at = pick(NOISE_AT)
    cot_at = pick(COT_AT)

    @pl.when(noise_at < 0)
    def _():
        send_noise()

    @pl.when(cot_at < 0)
    def _():
        send_cot()

    def send_states(to):
        @pl.when(to != tm)
        def _():
            remote(
                states.at[pl.ds(to * here, here)], states_hbm.at[:, strip(tm)], states_send, states_recv, (to, batch)
            )

    dot_[...] = do[...].T
    not_[...] = no[...].T
    dit[...] = di[...].T
    nit[...] = ni[...].T
    grads[...] = jnp.zeros_like(grads)
    bias_hidden[...] = jnp.zeros_like(bias_hidden)
    bias_out[...] = jnp.zeros_like(bias_out)
    begin_copy.wait()

    def sends(k):
        @pl.when(k == noise_at)
        def _():
            send_noise()

        @pl.when(k == cot_at)
        def _():
            send_cot()

    def forward_step(k, z):
        q = z.astype(BF)
        q_all[k] = q
        u = jnp.tanh(matmul(q, di[...]) + dh[...]).astype(BF)
        v = jnp.tanh(matmul(q, ni[...]) + nh[...]).astype(BF)
        u_all[k] = u
        v_all[k] = v
        drift = matmul(u, do[...])
        s = jax.nn.sigmoid(matmul(v, no[...]) + nof[...])
        s_all[k] = s
        z = z + delta_time * (drift + dof[...]) + s * noise[k]
        states[k] = z
        return z

    def fine_step(k, z):
        sends(k)
        wait_bytes(noise.at[k], fine_recv.at[k])
        return forward_step(k, z)

    def forward_section(g, z):
        sends(g * here)

        @pl.when(g == SECTIONS - 1)
        def _():
            send_states(0)
            send_states(1)

        wait_bytes(noise.at[pl.ds(g * here, here)], noise_recv.at[g])
        return lax.fori_loop(0, here, lambda m, z: forward_step(g * here + m, z), z)

    z = lax.fori_loop(0, FINE * here, fine_step, begin[...])
    lax.fori_loop(FINE, SECTIONS, forward_section, z)

    local(states.at[mine], states_hbm.at[:, strip(tm)], own.at[1])

    def fold(x):
        return jnp.sum(x.reshape(x.shape[0] // 8, 8, x.shape[1]), 0)

    def add(net, base, stride, value):
        for h in range(2):
            part = value[:, h * LANES : (h + 1) * LANES].reshape(chunk // 8, 8, LANES)
            at = pl.ds(base + h, chunk // 8, stride=stride)
            grads[net, at] = grads[net, at] + part

    def backward_section(t, e):
        g = SECTIONS - 1 - t
        section = pl.ds(g * here, here)

        @pl.when(t < SECTIONS // 2 - 1)
        def _():
            send_states(2 * t + 2)
            send_states(2 * t + 3)

        wait_bytes(cot.at[section], cot_recv.at[g])

        def step(back, e):
            m = here - 1 - back
            k = g * here + m
            w = e + cot[k]
            s = s_all[k]
            f = delta_time * w
            r0 = w * noise[k] * s * (1.0 - s)
            fb, gb = f.astype(BF), r0.astype(BF)
            fb_all[m] = fb
            gb_all[m] = gb
            bias_out[0] += fold(f)
            bias_out[1] += fold(r0)
            acc = w
            for c in range(CHUNKS):
                cols = slice(c * chunk, (c + 1) * chunk)
                u = u_all[k, :, cols].astype(F32)
                v = v_all[k, :, cols].astype(F32)
                p = matmul(fb, dot_[:, cols]) * (1.0 - u * u)
                r = matmul(gb, not_[:, cols]) * (1.0 - v * v)
                pb, rb = p.astype(BF), r.astype(BF)
                pb_all[m, :, cols] = pb
                rb_all[m, :, cols] = rb
                bias_hidden[0, :, cols] += fold(p)
                bias_hidden[1, :, cols] += fold(r)
                acc = acc + matmul(pb, dit[cols, :]) + matmul(rb, nit[cols, :])
            adjoints[k] = acc
            return acc

        e = lax.fori_loop(0, here, step, e)

        flat = here * rows
        q = q_all[section].reshape(flat, L)
        fb = fb_all[...].reshape(flat, L)
        gb = gb_all[...].reshape(flat, L)
        for c in range(CHUNKS):
            cols = slice(c * chunk, (c + 1) * chunk)
            add(0, 2 * c, H // LANES, matmul_rows(q, pb_all[:, :, cols].reshape(flat, chunk)))
            add(1, 2 * c, H // LANES, matmul_rows(q, rb_all[:, :, cols].reshape(flat, chunk)))
            add(0, INNER + c * chunk // 4, L // LANES, matmul_rows(u_all[section, :, cols].reshape(flat, chunk), fb))
            add(1, INNER + c * chunk // 4, L // LANES, matmul_rows(v_all[section, :, cols].reshape(flat, chunk), gb))

        @pl.when(g == tm)
        def _():
            local(adjoints.at[mine], adjoints_hbm.at[:, strip(tm)], own.at[2])

        @pl.when(g != tm)
        def _():
            remote(adjoints.at[section], adjoints_hbm.at[:, strip(tm)], adj_send, adj_recv, (g, batch))

        return e

    lax.fori_loop(0, SECTIONS, backward_section, jnp.zeros((rows, L), F32))

    for net in range(2):
        hidden = jnp.sum(bias_hidden[net], 0, keepdims=True)
        last = jnp.sum(bias_out[net], 0, keepdims=True)
        for j in range(H // LANES):
            grads[net, 2 * INNER, j : j + 1, :] = hidden[:, j * LANES : (j + 1) * LANES]
        for j in range(L // LANES):
            grads[net, 2 * INNER + 1, j : j + 1, :] = last[:, j * LANES : (j + 1) * LANES]

    landed = (landed1, landed2, landed3)
    parts = [[size // SIDE ** (phase + 1) for phase in range(3)] for size in SIZES]

    swaps = {}
    for color in EARLY + LATE:
        span = pl.ds(STARTS[color], SIZES[color])
        swaps[color] = remote(grads.at[other, span], held.at[span], sib_send.at[color], sib_recv.at[color], sibling)

    bases = list(STARTS)
    moves = {}
    started = []

    def scatter(color, phase):
        axis, part = ORDERS[color][phase], parts[color][phase]
        span = pl.ds(bases[color], part * SIDE)
        if phase == 0:
            swaps[color].wait_recv()
            held[span] = held[span] + grads[core, span]
        else:
            for move in moves[color]:
                move.wait_recv()
            got, whole = landed[phase - 1].at[color], pl.ds(0, part * SIDE)
            held[span] = held[span] + got[0, whole] + (got[1, whole] + got[2, whole])
        moves[color] = [
            remote(
                held.at[pl.ds(bases[color] + lax.rem(place[axis] + distance, SIDE) * part, part)],
                landed[phase].at[color, distance - 1, pl.ds(0, part)],
                send.at[color, phase, distance - 1],
                recv.at[color, phase, distance - 1],
                partner(axis, distance),
            )
            for distance in range(1, SIDE)
        ]
        started.extend(moves[color])
        bases[color] = bases[color] + place[axis] * part

    def gather(color, phase):
        axis, part = ORDERS[color][phase], parts[color][phase]
        span = pl.ds(bases[color], part)
        for move in moves[color]:
            move.wait_recv()
        if phase == 2:
            whole = pl.ds(0, part)
            got = landed3.at[color]
            out[core, span] = held[span] + got[0, whole] + (got[1, whole] + got[2, whole])
        moves[color] = [
            remote(
                out.at[core, span],
                out.at[core, span],
                send.at[color, 5 - phase, distance - 1],
                recv.at[color, 5 - phase, distance - 1],
                partner(axis, distance),
            )
            for distance in range(1, SIDE)
        ]
        started.extend(moves[color])
        if phase == 0:
            started.append(
                remote(out.at[core, span], out.at[core, span], back_send.at[color, 0], back_recv.at[color, 0], sibling)
            )
        bases[color] = bases[color] - place[axis] * part

    def give_back(color):
        axis, part = ORDERS[color][0], parts[color][0]
        for distance in range(1, SIDE):
            moves[color][distance - 1].wait_recv()
            source = lax.rem(place[axis] + SIDE - distance, SIDE)
            span = pl.ds(bases[color] + source * part, part)
            started.append(
                remote(
                    out.at[core, span], out.at[core, span],
                    back_send.at[color, distance], back_recv.at[color, distance], sibling,
                )
            )

    tasks = [
        lambda c: scatter(c, 0), lambda c: scatter(c, 1), lambda c: scatter(c, 2),
        lambda c: gather(c, 2), lambda c: gather(c, 1), lambda c: gather(c, 0), give_back,
    ]
    order = ((EARLY, 0), (LATE, 0), (EARLY, 1), (EARLY, 2), (EARLY, 3), (LATE, 1), (EARLY, 4),
             (LATE, 2), (EARLY, 5), (LATE, 3), (LATE, 4), (LATE, 5), (EARLY, 6), (LATE, 6))
    for colors, task in order:
        for color in colors:
            tasks[task](color)
    for color in range(COLORS):
        axis, part = ORDERS[color][0], parts[color][0]
        for distance in range(SIDE):
            source = lax.rem(place[axis] + SIDE - distance, SIDE)
            view = out.at[other, pl.ds(STARTS[color] + source * part, part)]
            pltpu.make_async_copy(view, view, back_recv.at[color, distance]).wait()
    total = jnp.zeros((8, LANES), F32)
    step = 64

    def squares(i, total):
        a, b = out[0, pl.ds(i * step, step)], out[1, pl.ds(i * step, step)]
        return total + jnp.sum(a * a + b * b, 0)

    total = lax.fori_loop(0, TILES // step, squares, total)
    total = jnp.sum(jnp.sum(total, 1, keepdims=True), 0, keepdims=True)
    factor[...] = jnp.broadcast_to(clip_factor(total), (8, LANES))
    for move in [*swaps.values(), *started]:
        move.wait_send()
    others = pl.ds(0, total_steps - here)
    for sem in (noise_send, cot_send, states_send, adj_send):
        wait_bytes(noise.at[others], sem)
    sent_rows = pl.ds(0, rows * (SECTIONS - 1))
    wait_bytes(states_hbm.at[:, sent_rows], states_recv)
    wait_bytes(adjoints_hbm.at[:, sent_rows], adj_recv)
    wait_bytes(states.at[mine], own.at[1])
    wait_bytes(states.at[mine], own.at[2])


def window(start, noise, cot, params):
    dma = pltpu.SemaphoreType.DMA
    here, wide, _ = noise.shape
    steps, rows = here * SECTIONS, wide // SECTIONS
    vmem = pl.BlockSpec(memory_space=pltpu.VMEM)
    anywhere = pl.BlockSpec(memory_space=pl.ANY)
    V = pltpu.VMEM
    sums = (2, TILES, 8, LANES)
    return pl.pallas_call(
        window_kernel,
        in_specs=[anywhere] * 3 + [vmem] * 8,
        out_specs=[anywhere] * 2 + [vmem] * 2,
        out_shape=[
            jax.ShapeDtypeStruct(noise.shape, F32),
            jax.ShapeDtypeStruct(noise.shape, F32),
            jax.ShapeDtypeStruct(sums, F32),
            jax.ShapeDtypeStruct((8, LANES), F32),
        ],
        scratch_shapes=[
            *(V((steps, rows, L), F32) for _ in range(4)),
            V((steps, rows, L), BF), V((steps, rows, H), BF), V((steps, rows, H), BF), V((steps, rows, L), F32),
            V((here, rows, H), BF), V((here, rows, H), BF), V((here, rows, L), BF), V((here, rows, L), BF),
            V((2, 8, H), F32), V((2, 8, L), F32), V((rows, L), F32),
            V((L, H), BF), V((H, L), BF), V((L, H), BF), V((H, L), BF),
            V(sums, F32),
            V((TILES, 8, LANES), F32),
            *(V((COLORS, 3, max(SIZES) // SIDE ** (p + 1), 8, LANES), F32) for p in range(3)),
            dma((3,)), dma, dma((SECTIONS,)), dma((FINE * here,)), dma, dma((SECTIONS,)), dma, dma, dma, dma,
            dma((COLORS,)), dma((COLORS,)),
            dma((COLORS, 6, 3)), dma((COLORS, 6, 3)),
            dma((COLORS, 4)), dma((COLORS, 4)),
        ],
        name="sde_window",
        compiler_params=pltpu.CompilerParams(
            collective_id=0, has_side_effects=True, vmem_limit_bytes=62 * 1024 * 1024
        ),
    )(start, noise, cot, *params)


def clip_factor(total):
    limit = 0.5 * math.sqrt(4 * L * H + 2 * H + 2 * L)
    return jnp.minimum(1.0, limit / jnp.sqrt(total))


def shards(
    initial_state, increments, cotangents,
    drift_inner, drift_hidden, drift_outer, drift_offset,
    noise_inner, noise_hidden, noise_outer, noise_offset,
):
    states, adjoints, summed, factor = window(
        initial_state,
        increments,
        cotangents,
        (
            drift_inner, drift_hidden[None], drift_outer, drift_offset[None],
            noise_inner, noise_hidden[None], noise_outer, noise_offset[None],
        ),
    )
    factor = factor[0, 0]

    def matrix(net, base, rows, columns):
        tiles = summed[net, base : base + INNER].reshape(rows // 8, columns // LANES, 8, LANES)
        return tiles.transpose(0, 2, 1, 3).reshape(rows, columns) * factor

    result = []
    for net in range(2):
        result += [
            matrix(net, 0, L, H),
            summed[net, 2 * INNER].reshape(H) * factor,
            matrix(net, INNER, H, L),
            summed[net, 2 * INNER + 1, : L // LANES].reshape(L) * factor,
        ]
    return (states, adjoints, *result)


def solution(mesh):
    split = P("tm", "batch", None)
    return jax.shard_map(
        shards,
        mesh=mesh,
        in_specs=(P("batch", None), split, split) + (P(),) * 8,
        out_specs=(split, split) + (P(),) * 8,
        check_vma=False,
    )
```

```python
import math

import jax
import jax.numpy as jnp
from jax import lax
from jax.experimental import pallas as pl
from jax.experimental.pallas import tpu as pltpu
from jax.sharding import PartitionSpec as P

L = 256
H = 1024
CHUNKS = 4
SECTIONS = 8
NOISE_AT = (-1, 5, 3, 8, -1, 2, 8, 16)
COT_AT = (16, 24, 40, 32, 24, 16, -1, -1)
FINE = 2
delta_time = 0.05
LANES = 128
INNER = L * H // (8 * LANES)
COLORS = 5
SIZES = (128, 128, 128, 128, 64)
STARTS = (0, 128, 256, 384, 512)
ORDERS = ((1, 2, 0), (2, 1, 0), (1, 2, 0), (2, 1, 0), (0, 1, 2))
EARLY, LATE = (0, 1), (2, 3, 4)
SIDE = 4
TILES = sum(SIZES)
MESH = pl.DeviceIdType.MESH
F32 = jnp.float32
BF = jnp.bfloat16


def matmul(left, right):
    return jnp.dot(left, right, preferred_element_type=F32)


def matmul_rows(left, right):
    return lax.dot_general(left, right, (((0,), (0,)), ((), ())), preferred_element_type=F32)


def window_kernel(
    start, noise_hbm, cot_hbm, di, dh, do, dof, ni, nh, no, nof,
    states_hbm, adjoints_hbm, out, factor,
    noise, cot, states, adjoints, q_all, u_all, v_all, s_all,
    pb_all, rb_all, fb_all, gb_all, bias_hidden, bias_out, begin,
    dot_, dit, not_, nit, grads, held, landed1, landed2, landed3,
    own, noise_send, noise_recv, fine_recv, cot_send, cot_recv, states_send, states_recv, adj_send, adj_recv,
    sib_send, sib_recv, send, recv, back_send, back_recv,
):
    tm = lax.axis_index("tm")
    batch = lax.axis_index("batch")
    core = lax.rem(tm, 2)
    place = (lax.div(tm, 2), lax.div(batch, SIDE), lax.rem(batch, SIDE))
    other = 1 - core
    sibling = (tm + 1 - 2 * core, batch)
    here = noise_hbm.shape[0]
    rows = noise_hbm.shape[1] // SECTIONS
    total_steps = here * SECTIONS
    chunk = H // CHUNKS

    def partner(axis, distance):
        moved = lax.rem(place[axis] + distance, SIDE)
        x, y, z = (moved if a == axis else place[a] for a in range(3))
        return (2 * x + core, SIDE * y + z)

    def pick(table):
        chosen = jnp.int32(table[0])
        for index in range(1, len(table)):
            chosen = jnp.where(tm == index, table[index], chosen)
        return chosen

    def strip(index):
        return pl.ds(pl.multiple_of(index * rows, rows), rows)

    def remote(src, dst, send_sem, recv_sem, device):
        copy = pltpu.make_async_remote_copy(
            src_ref=src, dst_ref=dst, send_sem=send_sem, recv_sem=recv_sem, device_id=device, device_id_type=MESH
        )
        copy.start()
        return copy

    def local(src, dst, sem):
        copy = pltpu.make_async_copy(src, dst, sem)
        copy.start()
        return copy

    def wait_bytes(view, sem):
        pltpu.make_async_copy(view, view, sem).wait()

    begin_copy = local(start.at[strip(tm)], begin, own.at[0])

    mine = pl.ds(tm * here, here)

    @pl.when(tm < FINE)
    def _():
        def own_noise(m, _):
            k = tm * here + m
            local(noise_hbm.at[m, strip(tm)], noise.at[k], fine_recv.at[k])
            return 0

        lax.fori_loop(0, here, own_noise, 0)

    @pl.when(tm >= FINE)
    def _():
        local(noise_hbm.at[:, strip(tm)], noise.at[mine], noise_recv.at[tm])

    local(cot_hbm.at[:, strip(tm)], cot.at[mine], cot_recv.at[tm])

    barrier = pltpu.get_barrier_semaphore()
    for distance in range(1, SECTIONS):
        pl.semaphore_signal(
            barrier, inc=1, device_id=(lax.rem(tm + distance, SECTIONS), batch), device_id_type=MESH
        )
    for axis in (1, 2):
        for distance in range(1, SIDE):
            pl.semaphore_signal(barrier, inc=1, device_id=partner(axis, distance), device_id_type=MESH)
    pl.semaphore_wait(barrier, 13)

    def send_noise():
        @pl.when(tm < FINE)
        def _():
            def each(m, _):
                k = tm * here + m
                for distance in range(1, SECTIONS):
                    to = lax.rem(tm + distance, SECTIONS)
                    remote(noise_hbm.at[m, strip(to)], noise.at[k], noise_send, fine_recv.at[k], (to, batch))
                return 0

            lax.fori_loop(0, here, each, 0)

        @pl.when(tm >= FINE)
        def _():
            for distance in range(1, SECTIONS):
                to = lax.rem(tm + distance, SECTIONS)
                remote(noise_hbm.at[:, strip(to)], noise.at[mine], noise_send, noise_recv.at[tm], (to, batch))

    def send_cot():
        for distance in range(1, SECTIONS):
            to = lax.rem(tm + distance, SECTIONS)
            remote(cot_hbm.at[:, strip(to)], cot.at[mine], cot_send, cot_recv.at[tm], (to, batch))

    noise_at = pick(NOISE_AT)
    cot_at = pick(COT_AT)

    @pl.when(noise_at < 0)
    def _():
        send_noise()

    @pl.when(cot_at < 0)
    def _():
        send_cot()

    def send_states(to):
        @pl.when(to != tm)
        def _():
            remote(
                states.at[pl.ds(to * here, here)], states_hbm.at[:, strip(tm)], states_send, states_recv, (to, batch)
            )

    dot_[...] = do[...].T
    not_[...] = no[...].T
    dit[...] = di[...].T
    nit[...] = ni[...].T
    grads[...] = jnp.zeros_like(grads)
    bias_hidden[...] = jnp.zeros_like(bias_hidden)
    bias_out[...] = jnp.zeros_like(bias_out)
    begin_copy.wait()

    def sends(k):
        @pl.when(k == noise_at)
        def _():
            send_noise()

        @pl.when(k == cot_at)
        def _():
            send_cot()

    def forward_step(k, z):
        q = z.astype(BF)
        q_all[k] = q
        u = jnp.tanh(matmul(q, di[...]) + dh[...]).astype(BF)
        v = jnp.tanh(matmul(q, ni[...]) + nh[...]).astype(BF)
        u_all[k] = u
        v_all[k] = v
        drift = matmul(u, do[...])
        s = jax.nn.sigmoid(matmul(v, no[...]) + nof[...])
        s_all[k] = s
        z = z + delta_time * (drift + dof[...]) + s * noise[k]
        states[k] = z
        return z

    def fine_step(k, z):
        sends(k)
        wait_bytes(noise.at[k], fine_recv.at[k])
        return forward_step(k, z)

    def forward_section(g, z):
        sends(g * here)

        @pl.when(g == SECTIONS - 1)
        def _():
            send_states(0)
            send_states(1)

        wait_bytes(noise.at[pl.ds(g * here, here)], noise_recv.at[g])
        return lax.fori_loop(0, here, lambda m, z: forward_step(g * here + m, z), z)

    z = lax.fori_loop(0, FINE * here, fine_step, begin[...])
    lax.fori_loop(FINE, SECTIONS, forward_section, z)

    local(states.at[mine], states_hbm.at[:, strip(tm)], own.at[1])

    def fold(x):
        return jnp.sum(x.reshape(x.shape[0] // 8, 8, x.shape[1]), 0)

    def add(net, base, stride, value):
        for h in range(2):
            part = value[:, h * LANES : (h + 1) * LANES].reshape(chunk // 8, 8, LANES)
            at = pl.ds(base + h, chunk // 8, stride=stride)
            grads[net, at] = grads[net, at] + part

    def backward_section(t, e):
        g = SECTIONS - 1 - t
        section = pl.ds(g * here, here)

        @pl.when(t < SECTIONS // 2 - 1)
        def _():
            send_states(2 * t + 2)
            send_states(2 * t + 3)

        wait_bytes(cot.at[section], cot_recv.at[g])

        def step(back, e):
            m = here - 1 - back
            k = g * here + m
            w = e + cot[k]
            s = s_all[k]
            f = delta_time * w
            r0 = w * noise[k] * s * (1.0 - s)
            fb, gb = f.astype(BF), r0.astype(BF)
            fb_all[m] = fb
            gb_all[m] = gb
            bias_out[0] += fold(f)
            bias_out[1] += fold(r0)
            acc = w
            for c in range(CHUNKS):
                cols = slice(c * chunk, (c + 1) * chunk)
                u = u_all[k, :, cols].astype(F32)
                v = v_all[k, :, cols].astype(F32)
                p = matmul(fb, dot_[:, cols]) * (1.0 - u * u)
                r = matmul(gb, not_[:, cols]) * (1.0 - v * v)
                pb, rb = p.astype(BF), r.astype(BF)
                pb_all[m, :, cols] = pb
                rb_all[m, :, cols] = rb
                bias_hidden[0, :, cols] += fold(p)
                bias_hidden[1, :, cols] += fold(r)
                acc = acc + matmul(pb, dit[cols, :]) + matmul(rb, nit[cols, :])
            adjoints[k] = acc
            return acc

        e = lax.fori_loop(0, here, step, e)

        flat = here * rows
        q = q_all[section].reshape(flat, L)
        fb = fb_all[...].reshape(flat, L)
        gb = gb_all[...].reshape(flat, L)
        for c in range(CHUNKS):
            cols = slice(c * chunk, (c + 1) * chunk)
            add(0, 2 * c, H // LANES, matmul_rows(q, pb_all[:, :, cols].reshape(flat, chunk)))
            add(1, 2 * c, H // LANES, matmul_rows(q, rb_all[:, :, cols].reshape(flat, chunk)))
            add(0, INNER + c * chunk // 4, L // LANES, matmul_rows(u_all[section, :, cols].reshape(flat, chunk), fb))
            add(1, INNER + c * chunk // 4, L // LANES, matmul_rows(v_all[section, :, cols].reshape(flat, chunk), gb))

        @pl.when(g == tm)
        def _():
            local(adjoints.at[mine], adjoints_hbm.at[:, strip(tm)], own.at[2])

        @pl.when(g != tm)
        def _():
            remote(adjoints.at[section], adjoints_hbm.at[:, strip(tm)], adj_send, adj_recv, (g, batch))

        return e

    lax.fori_loop(0, SECTIONS, backward_section, jnp.zeros((rows, L), F32))

    for net in range(2):
        hidden = jnp.sum(bias_hidden[net], 0, keepdims=True)
        last = jnp.sum(bias_out[net], 0, keepdims=True)
        for j in range(H // LANES):
            grads[net, 2 * INNER, j : j + 1, :] = hidden[:, j * LANES : (j + 1) * LANES]
        for j in range(L // LANES):
            grads[net, 2 * INNER + 1, j : j + 1, :] = last[:, j * LANES : (j + 1) * LANES]

    landed = (landed1, landed2, landed3)
    parts = [[size // SIDE ** (phase + 1) for phase in range(3)] for size in SIZES]

    swaps = {}
    for color in EARLY + LATE:
        span = pl.ds(STARTS[color], SIZES[color])
        swaps[color] = remote(grads.at[other, span], held.at[span], sib_send.at[color], sib_recv.at[color], sibling)

    bases = list(STARTS)
    moves = {}
    started = []

    def scatter(color, phase):
        axis, part = ORDERS[color][phase], parts[color][phase]
        span = pl.ds(bases[color], part * SIDE)
        if phase == 0:
            swaps[color].wait_recv()
            held[span] = held[span] + grads[core, span]
        else:
            for move in moves[color]:
                move.wait_recv()
            got, whole = landed[phase - 1].at[color], pl.ds(0, part * SIDE)
            held[span] = held[span] + got[0, whole] + (got[1, whole] + got[2, whole])
        moves[color] = [
            remote(
                held.at[pl.ds(bases[color] + lax.rem(place[axis] + distance, SIDE) * part, part)],
                landed[phase].at[color, distance - 1, pl.ds(0, part)],
                send.at[color, phase, distance - 1],
                recv.at[color, phase, distance - 1],
                partner(axis, distance),
            )
            for distance in range(1, SIDE)
        ]
        started.extend(moves[color])
        bases[color] = bases[color] + place[axis] * part

    def gather(color, phase):
        axis, part = ORDERS[color][phase], parts[color][phase]
        span = pl.ds(bases[color], part)
        for move in moves[color]:
            move.wait_recv()
        if phase == 2:
            whole = pl.ds(0, part)
            got = landed3.at[color]
            out[core, span] = held[span] + got[0, whole] + (got[1, whole] + got[2, whole])
        moves[color] = [
            remote(
                out.at[core, span],
                out.at[core, span],
                send.at[color, 5 - phase, distance - 1],
                recv.at[color, 5 - phase, distance - 1],
                partner(axis, distance),
            )
            for distance in range(1, SIDE)
        ]
        started.extend(moves[color])
        if phase == 0:
            started.append(
                remote(out.at[core, span], out.at[core, span], back_send.at[color, 0], back_recv.at[color, 0], sibling)
            )
        bases[color] = bases[color] - place[axis] * part

    def give_back(color):
        axis, part = ORDERS[color][0], parts[color][0]
        for distance in range(1, SIDE):
            moves[color][distance - 1].wait_recv()
            source = lax.rem(place[axis] + SIDE - distance, SIDE)
            span = pl.ds(bases[color] + source * part, part)
            started.append(
                remote(
                    out.at[core, span], out.at[core, span],
                    back_send.at[color, distance], back_recv.at[color, distance], sibling,
                )
            )

    tasks = [
        lambda c: scatter(c, 0), lambda c: scatter(c, 1), lambda c: scatter(c, 2),
        lambda c: gather(c, 2), lambda c: gather(c, 1), lambda c: gather(c, 0), give_back,
    ]
    order = ((EARLY, 0), (LATE, 0), (EARLY, 1), (EARLY, 2), (EARLY, 3), (LATE, 1), (EARLY, 4),
             (LATE, 2), (EARLY, 5), (LATE, 3), (LATE, 4), (LATE, 5), (EARLY, 6), (LATE, 6))
    for colors, task in order:
        for color in colors:
            tasks[task](color)
    for color in range(COLORS):
        axis, part = ORDERS[color][0], parts[color][0]
        for distance in range(SIDE):
            source = lax.rem(place[axis] + SIDE - distance, SIDE)
            view = out.at[other, pl.ds(STARTS[color] + source * part, part)]
            pltpu.make_async_copy(view, view, back_recv.at[color, distance]).wait()
    total = jnp.zeros((8, LANES), F32)
    step = 64

    def squares(i, total):
        a, b = out[0, pl.ds(i * step, step)], out[1, pl.ds(i * step, step)]
        return total + jnp.sum(a * a + b * b, 0)

    total = lax.fori_loop(0, TILES // step, squares, total)
    total = jnp.sum(jnp.sum(total, 1, keepdims=True), 0, keepdims=True)
    factor[...] = jnp.broadcast_to(clip_factor(total), (8, LANES))
    for move in [*swaps.values(), *started]:
        move.wait_send()
    others = pl.ds(0, total_steps - here)
    for sem in (noise_send, cot_send, states_send, adj_send):
        wait_bytes(noise.at[others], sem)
    sent_rows = pl.ds(0, rows * (SECTIONS - 1))
    wait_bytes(states_hbm.at[:, sent_rows], states_recv)
    wait_bytes(adjoints_hbm.at[:, sent_rows], adj_recv)
    wait_bytes(states.at[mine], own.at[1])
    wait_bytes(states.at[mine], own.at[2])


def window(start, noise, cot, params):
    dma = pltpu.SemaphoreType.DMA
    here, wide, _ = noise.shape
    steps, rows = here * SECTIONS, wide // SECTIONS
    vmem = pl.BlockSpec(memory_space=pltpu.VMEM)
    anywhere = pl.BlockSpec(memory_space=pl.ANY)
    V = pltpu.VMEM
    sums = (2, TILES, 8, LANES)
    return pl.pallas_call(
        window_kernel,
        in_specs=[anywhere] * 3 + [vmem] * 8,
        out_specs=[anywhere] * 2 + [vmem] * 2,
        out_shape=[
            jax.ShapeDtypeStruct(noise.shape, F32),
            jax.ShapeDtypeStruct(noise.shape, F32),
            jax.ShapeDtypeStruct(sums, F32),
            jax.ShapeDtypeStruct((8, LANES), F32),
        ],
        scratch_shapes=[
            *(V((steps, rows, L), F32) for _ in range(4)),
            V((steps, rows, L), BF), V((steps, rows, H), BF), V((steps, rows, H), BF), V((steps, rows, L), F32),
            V((here, rows, H), BF), V((here, rows, H), BF), V((here, rows, L), BF), V((here, rows, L), BF),
            V((2, 8, H), F32), V((2, 8, L), F32), V((rows, L), F32),
            V((L, H), BF), V((H, L), BF), V((L, H), BF), V((H, L), BF),
            V(sums, F32),
            V((TILES, 8, LANES), F32),
            *(V((COLORS, 3, max(SIZES) // SIDE ** (p + 1), 8, LANES), F32) for p in range(3)),
            dma((3,)), dma, dma((SECTIONS,)), dma((FINE * here,)), dma, dma((SECTIONS,)), dma, dma, dma, dma,
            dma((COLORS,)), dma((COLORS,)),
            dma((COLORS, 6, 3)), dma((COLORS, 6, 3)),
            dma((COLORS, 4)), dma((COLORS, 4)),
        ],
        name="sde_window",
        compiler_params=pltpu.CompilerParams(
            collective_id=0, has_side_effects=True, vmem_limit_bytes=62 * 1024 * 1024
        ),
    )(start, noise, cot, *params)


def finish_kernel(
    states, adjoints, di, do, ni, no, drift_bias, noise_bias, factor,
    states_out, adjoints_out, di_out, dh_out, do_out, dof_out, ni_out, nh_out, no_out, nof_out,
):
    states_out[...] = states[...]
    adjoints_out[...] = adjoints[...]
    scale = factor[...]

    def spread(tiles, matrix):
        rows, columns = matrix.shape
        wide = columns // LANES
        for i in range(rows // 8):
            for j in range(wide):
                matrix[8 * i : 8 * i + 8, j * LANES : (j + 1) * LANES] = tiles[0, i * wide + j] * scale

    spread(di, di_out)
    spread(do, do_out)
    spread(ni, ni_out)
    spread(no, no_out)
    for tiles, hidden, last in ((drift_bias, dh_out, dof_out), (noise_bias, nh_out, nof_out)):
        for out, tile in ((hidden, tiles[0, 0] * scale), (last, tiles[0, 1] * scale)):
            for j in range(out.shape[1] // LANES):
                out[:, j * LANES : (j + 1) * LANES] = tile[j : j + 1, :]


def finish(states, adjoints, summed, factor):
    here, wide, _ = states.shape
    pieces = INNER // (INNER // here)
    tiles = INNER // pieces
    bias = 2 * INNER // tiles

    def matrix(net, base):
        return pl.BlockSpec((1, tiles, 8, LANES), lambda g: (net, base // tiles + g, 0, 0))

    def biases(net):
        return pl.BlockSpec((1, tiles, 8, LANES), lambda g: (net, bias, 0, 0))

    part = pl.BlockSpec((1, wide, L), lambda g: (g, 0, 0))
    inner = pl.BlockSpec((L // pieces, H), lambda g: (g, 0))
    outer = pl.BlockSpec((H // pieces, L), lambda g: (g, 0))

    def row(width):
        return pl.BlockSpec((1, width), lambda g: (0, 0))

    def shape(*dims):
        return jax.ShapeDtypeStruct(dims, F32)

    results = pl.pallas_call(
        finish_kernel,
        grid=(pieces,),
        in_specs=[
            part, part, matrix(0, 0), matrix(0, INNER), matrix(1, 0), matrix(1, INNER), biases(0), biases(1),
            pl.BlockSpec((8, LANES), lambda g: (0, 0)),
        ],
        out_specs=[part, part] + [inner, row(H), outer, row(L)] * 2,
        out_shape=[shape(*states.shape)] * 2 + [shape(L, H), shape(1, H), shape(H, L), shape(1, L)] * 2,
        name="sde_finish",
    )(states, adjoints, *(summed,) * 6, factor)
    return tuple(r.reshape(-1) if r.shape[0] == 1 else r for r in results)


def clip_factor(total):
    limit = 0.5 * math.sqrt(4 * L * H + 2 * H + 2 * L)
    return jnp.minimum(1.0, limit / jnp.sqrt(total))


def shards(
    initial_state, increments, cotangents,
    drift_inner, drift_hidden, drift_outer, drift_offset,
    noise_inner, noise_hidden, noise_outer, noise_offset,
):
    states, adjoints, summed, factor = window(
        initial_state,
        increments,
        cotangents,
        (
            drift_inner, drift_hidden[None], drift_outer, drift_offset[None],
            noise_inner, noise_hidden[None], noise_outer, noise_offset[None],
        ),
    )

    return finish(states, adjoints, summed, factor)


def solution(mesh):
    split = P("tm", "batch", None)
    return jax.shard_map(
        shards,
        mesh=mesh,
        in_specs=(P("batch", None), split, split) + (P(),) * 8,
        out_specs=(split, split) + (P(),) * 8,
        check_vma=False,
    )
```

```python
import math

import jax
import jax.numpy as jnp
from jax import lax
from jax.experimental import pallas as pl
from jax.experimental.pallas import tpu as pltpu
from jax.sharding import PartitionSpec as P

L = 256
H = 1024
CHUNKS = 4
SECTIONS = 8
NOISE_AT = (-1, 5, 3, 8, -1, 2, 8, 16)
COT_AT = (16, 24, 40, 32, 24, 16, -1, -1)
FINE = 2
delta_time = 0.05
LANES = 128
INNER = L * H // (8 * LANES)
COLORS = 5
SIZES = (128, 128, 128, 128, 64)
STARTS = (0, 128, 256, 384, 512)
ORDERS = ((1, 2, 0), (2, 1, 0), (1, 2, 0), (2, 1, 0), (0, 1, 2))
EARLY, LATE = (0, 1), (2, 3, 4)
SIDE = 4
TILES = sum(SIZES)
MESH = pl.DeviceIdType.MESH
F32 = jnp.float32
BF = jnp.bfloat16


def matmul(left, right):
    return jnp.dot(left, right, preferred_element_type=F32)


def matmul_rows(left, right):
    return lax.dot_general(left, right, (((0,), (0,)), ((), ())), preferred_element_type=F32)


def window_kernel(
    start, noise_hbm, cot_hbm, di, dh, do, dof, ni, nh, no, nof,
    states_hbm, adjoints_hbm, out, factor,
    noise, cot, states, adjoints, q_all, u_all, v_all, s_all,
    pb_all, rb_all, fb_all, gb_all, bias_hidden, bias_out, begin,
    dot_, dit, not_, nit, grads, held, landed1, landed2, landed3,
    own, noise_send, noise_recv, fine_recv, cot_send, cot_recv, states_send, states_recv, adj_send, adj_recv,
    sib_send, sib_recv, send, recv, back_send, back_recv,
):
    tm = lax.axis_index("tm")
    batch = lax.axis_index("batch")
    core = lax.rem(tm, 2)
    place = (lax.div(tm, 2), lax.div(batch, SIDE), lax.rem(batch, SIDE))
    other = 1 - core
    sibling = (tm + 1 - 2 * core, batch)
    here = noise_hbm.shape[0]
    rows = noise_hbm.shape[1] // SECTIONS
    total_steps = here * SECTIONS
    chunk = H // CHUNKS

    def partner(axis, distance):
        moved = lax.rem(place[axis] + distance, SIDE)
        x, y, z = (moved if a == axis else place[a] for a in range(3))
        return (2 * x + core, SIDE * y + z)

    def pick(table):
        chosen = jnp.int32(table[0])
        for index in range(1, len(table)):
            chosen = jnp.where(tm == index, table[index], chosen)
        return chosen

    def strip(index):
        return pl.ds(pl.multiple_of(index * rows, rows), rows)

    def remote(src, dst, send_sem, recv_sem, device):
        copy = pltpu.make_async_remote_copy(
            src_ref=src, dst_ref=dst, send_sem=send_sem, recv_sem=recv_sem, device_id=device, device_id_type=MESH
        )
        copy.start()
        return copy

    def local(src, dst, sem):
        copy = pltpu.make_async_copy(src, dst, sem)
        copy.start()
        return copy

    def wait_bytes(view, sem):
        pltpu.make_async_copy(view, view, sem).wait()

    begin_copy = local(start.at[strip(tm)], begin, own.at[0])

    mine = pl.ds(tm * here, here)

    @pl.when(tm < FINE)
    def _():
        def own_noise(m, _):
            k = tm * here + m
            local(noise_hbm.at[m, strip(tm)], noise.at[k], fine_recv.at[k])
            return 0

        lax.fori_loop(0, here, own_noise, 0)

    @pl.when(tm >= FINE)
    def _():
        local(noise_hbm.at[:, strip(tm)], noise.at[mine], noise_recv.at[tm])

    local(cot_hbm.at[:, strip(tm)], cot.at[mine], cot_recv.at[tm])

    barrier = pltpu.get_barrier_semaphore()
    for distance in range(1, SECTIONS):
        pl.semaphore_signal(
            barrier, inc=1, device_id=(lax.rem(tm + distance, SECTIONS), batch), device_id_type=MESH
        )
    for axis in (1, 2):
        for distance in range(1, SIDE):
            pl.semaphore_signal(barrier, inc=1, device_id=partner(axis, distance), device_id_type=MESH)
    pl.semaphore_wait(barrier, 13)

    def send_noise():
        @pl.when(tm < FINE)
        def _():
            def each(m, _):
                k = tm * here + m
                for distance in range(1, SECTIONS):
                    to = lax.rem(tm + distance, SECTIONS)
                    remote(noise_hbm.at[m, strip(to)], noise.at[k], noise_send, fine_recv.at[k], (to, batch))
                return 0

            lax.fori_loop(0, here, each, 0)

        @pl.when(tm >= FINE)
        def _():
            for distance in range(1, SECTIONS):
                to = lax.rem(tm + distance, SECTIONS)
                remote(noise_hbm.at[:, strip(to)], noise.at[mine], noise_send, noise_recv.at[tm], (to, batch))

    def send_cot():
        for distance in range(1, SECTIONS):
            to = lax.rem(tm + distance, SECTIONS)
            remote(cot_hbm.at[:, strip(to)], cot.at[mine], cot_send, cot_recv.at[tm], (to, batch))

    noise_at = pick(NOISE_AT)
    cot_at = pick(COT_AT)

    @pl.when(noise_at < 0)
    def _():
        send_noise()

    @pl.when(cot_at < 0)
    def _():
        send_cot()

    def send_states(to):
        @pl.when(to != tm)
        def _():
            remote(
                states.at[pl.ds(to * here, here)], states_hbm.at[:, strip(tm)], states_send, states_recv, (to, batch)
            )

    dot_[...] = do[...].T
    not_[...] = no[...].T
    dit[...] = di[...].T
    nit[...] = ni[...].T
    grads[...] = jnp.zeros_like(grads)
    bias_hidden[...] = jnp.zeros_like(bias_hidden)
    bias_out[...] = jnp.zeros_like(bias_out)
    begin_copy.wait()

    def sends(k):
        @pl.when(k == noise_at)
        def _():
            send_noise()

        @pl.when(k == cot_at)
        def _():
            send_cot()

    def forward_step(k, z):
        q = z.astype(BF)
        q_all[k] = q
        u = jnp.tanh(matmul(q, di[...]) + dh[...]).astype(BF)
        v = jnp.tanh(matmul(q, ni[...]) + nh[...]).astype(BF)
        u_all[k] = u
        v_all[k] = v
        drift = matmul(u, do[...])
        s = jax.nn.sigmoid(matmul(v, no[...]) + nof[...])
        s_all[k] = s
        z = z + delta_time * (drift + dof[...]) + s * noise[k]
        states[k] = z
        return z

    def fine_step(k, z):
        sends(k)
        wait_bytes(noise.at[k], fine_recv.at[k])
        return forward_step(k, z)

    def forward_section(g, z):
        sends(g * here)

        @pl.when(g == SECTIONS - 3)
        def _():
            send_states(0)
            send_states(1)

        @pl.when(g == SECTIONS - 1)
        def _():
            send_states(2)
            send_states(3)

        wait_bytes(noise.at[pl.ds(g * here, here)], noise_recv.at[g])
        return lax.fori_loop(0, here, lambda m, z: forward_step(g * here + m, z), z)

    z = lax.fori_loop(0, FINE * here, fine_step, begin[...])
    lax.fori_loop(FINE, SECTIONS, forward_section, z)

    local(states.at[mine], states_hbm.at[:, strip(tm)], own.at[1])

    def fold(x):
        return jnp.sum(x.reshape(x.shape[0] // 8, 8, x.shape[1]), 0)

    def add(net, base, stride, value):
        for h in range(2):
            part = value[:, h * LANES : (h + 1) * LANES].reshape(chunk // 8, 8, LANES)
            at = pl.ds(base + h, chunk // 8, stride=stride)
            grads[net, at] = grads[net, at] + part

    def backward_section(t, e):
        g = SECTIONS - 1 - t
        section = pl.ds(g * here, here)

        @pl.when(t < SECTIONS // 2 - 2)
        def _():
            send_states(2 * t + 4)
            send_states(2 * t + 5)

        wait_bytes(cot.at[section], cot_recv.at[g])

        def step(back, e):
            m = here - 1 - back
            k = g * here + m
            w = e + cot[k]
            s = s_all[k]
            f = delta_time * w
            r0 = w * noise[k] * s * (1.0 - s)
            fb, gb = f.astype(BF), r0.astype(BF)
            fb_all[m] = fb
            gb_all[m] = gb
            bias_out[0] += fold(f)
            bias_out[1] += fold(r0)
            acc = w
            for c in range(CHUNKS):
                cols = slice(c * chunk, (c + 1) * chunk)
                u = u_all[k, :, cols].astype(F32)
                v = v_all[k, :, cols].astype(F32)
                p = matmul(fb, dot_[:, cols]) * (1.0 - u * u)
                r = matmul(gb, not_[:, cols]) * (1.0 - v * v)
                pb, rb = p.astype(BF), r.astype(BF)
                pb_all[m, :, cols] = pb
                rb_all[m, :, cols] = rb
                bias_hidden[0, :, cols] += fold(p)
                bias_hidden[1, :, cols] += fold(r)
                acc = acc + matmul(pb, dit[cols, :]) + matmul(rb, nit[cols, :])
            adjoints[k] = acc
            return acc

        e = lax.fori_loop(0, here, step, e)

        flat = here * rows
        q = q_all[section].reshape(flat, L)
        fb = fb_all[...].reshape(flat, L)
        gb = gb_all[...].reshape(flat, L)
        for c in range(CHUNKS):
            cols = slice(c * chunk, (c + 1) * chunk)
            add(0, 2 * c, H // LANES, matmul_rows(q, pb_all[:, :, cols].reshape(flat, chunk)))
            add(1, 2 * c, H // LANES, matmul_rows(q, rb_all[:, :, cols].reshape(flat, chunk)))
            add(0, INNER + c * chunk // 4, L // LANES, matmul_rows(u_all[section, :, cols].reshape(flat, chunk), fb))
            add(1, INNER + c * chunk // 4, L // LANES, matmul_rows(v_all[section, :, cols].reshape(flat, chunk), gb))

        @pl.when(g == tm)
        def _():
            local(adjoints.at[mine], adjoints_hbm.at[:, strip(tm)], own.at[2])

        @pl.when(g != tm)
        def _():
            remote(adjoints.at[section], adjoints_hbm.at[:, strip(tm)], adj_send, adj_recv, (g, batch))

        return e

    lax.fori_loop(0, SECTIONS, backward_section, jnp.zeros((rows, L), F32))

    for net in range(2):
        hidden = jnp.sum(bias_hidden[net], 0, keepdims=True)
        last = jnp.sum(bias_out[net], 0, keepdims=True)
        for j in range(H // LANES):
            grads[net, 2 * INNER, j : j + 1, :] = hidden[:, j * LANES : (j + 1) * LANES]
        for j in range(L // LANES):
            grads[net, 2 * INNER + 1, j : j + 1, :] = last[:, j * LANES : (j + 1) * LANES]

    landed = (landed1, landed2, landed3)
    parts = [[size // SIDE ** (phase + 1) for phase in range(3)] for size in SIZES]

    swaps = {}
    for color in EARLY + LATE:
        span = pl.ds(STARTS[color], SIZES[color])
        swaps[color] = remote(grads.at[other, span], held.at[span], sib_send.at[color], sib_recv.at[color], sibling)

    bases = list(STARTS)
    moves = {}
    started = []

    def scatter(color, phase):
        axis, part = ORDERS[color][phase], parts[color][phase]
        span = pl.ds(bases[color], part * SIDE)
        if phase == 0:
            swaps[color].wait_recv()
            held[span] = held[span] + grads[core, span]
        else:
            for move in moves[color]:
                move.wait_recv()
            got, whole = landed[phase - 1].at[color], pl.ds(0, part * SIDE)
            held[span] = held[span] + got[0, whole] + (got[1, whole] + got[2, whole])
        moves[color] = [
            remote(
                held.at[pl.ds(bases[color] + lax.rem(place[axis] + distance, SIDE) * part, part)],
                landed[phase].at[color, distance - 1, pl.ds(0, part)],
                send.at[color, phase, distance - 1],
                recv.at[color, phase, distance - 1],
                partner(axis, distance),
            )
            for distance in range(1, SIDE)
        ]
        started.extend(moves[color])
        bases[color] = bases[color] + place[axis] * part

    def gather(color, phase):
        axis, part = ORDERS[color][phase], parts[color][phase]
        span = pl.ds(bases[color], part)
        for move in moves[color]:
            move.wait_recv()
        if phase == 2:
            whole = pl.ds(0, part)
            got = landed3.at[color]
            out[core, span] = held[span] + got[0, whole] + (got[1, whole] + got[2, whole])
        moves[color] = [
            remote(
                out.at[core, span],
                out.at[core, span],
                send.at[color, 5 - phase, distance - 1],
                recv.at[color, 5 - phase, distance - 1],
                partner(axis, distance),
            )
            for distance in range(1, SIDE)
        ]
        started.extend(moves[color])
        if phase == 0:
            started.append(
                remote(out.at[core, span], out.at[core, span], back_send.at[color, 0], back_recv.at[color, 0], sibling)
            )
        bases[color] = bases[color] - place[axis] * part

    def give_back(color):
        axis, part = ORDERS[color][0], parts[color][0]
        for distance in range(1, SIDE):
            moves[color][distance - 1].wait_recv()
            source = lax.rem(place[axis] + SIDE - distance, SIDE)
            span = pl.ds(bases[color] + source * part, part)
            started.append(
                remote(
                    out.at[core, span], out.at[core, span],
                    back_send.at[color, distance], back_recv.at[color, distance], sibling,
                )
            )

    tasks = [
        lambda c: scatter(c, 0), lambda c: scatter(c, 1), lambda c: scatter(c, 2),
        lambda c: gather(c, 2), lambda c: gather(c, 1), lambda c: gather(c, 0), give_back,
    ]
    order = ((EARLY, 0), (LATE, 0), (EARLY, 1), (EARLY, 2), (EARLY, 3), (LATE, 1), (EARLY, 4),
             (LATE, 2), (EARLY, 5), (LATE, 3), (LATE, 4), (LATE, 5), (EARLY, 6), (LATE, 6))
    for colors, task in order:
        for color in colors:
            tasks[task](color)
    for color in range(COLORS):
        axis, part = ORDERS[color][0], parts[color][0]
        for distance in range(SIDE):
            source = lax.rem(place[axis] + SIDE - distance, SIDE)
            view = out.at[other, pl.ds(STARTS[color] + source * part, part)]
            pltpu.make_async_copy(view, view, back_recv.at[color, distance]).wait()
    total = jnp.zeros((8, LANES), F32)
    step = 64

    def squares(i, total):
        a, b = out[0, pl.ds(i * step, step)], out[1, pl.ds(i * step, step)]
        return total + jnp.sum(a * a + b * b, 0)

    total = lax.fori_loop(0, TILES // step, squares, total)
    total = jnp.sum(jnp.sum(total, 1, keepdims=True), 0, keepdims=True)
    factor[...] = jnp.broadcast_to(clip_factor(total), (8, LANES))
    for move in [*swaps.values(), *started]:
        move.wait_send()
    others = pl.ds(0, total_steps - here)
    for sem in (noise_send, cot_send, states_send, adj_send):
        wait_bytes(noise.at[others], sem)
    sent_rows = pl.ds(0, rows * (SECTIONS - 1))
    wait_bytes(states_hbm.at[:, sent_rows], states_recv)
    wait_bytes(adjoints_hbm.at[:, sent_rows], adj_recv)
    wait_bytes(states.at[mine], own.at[1])
    wait_bytes(states.at[mine], own.at[2])


def window(start, noise, cot, params):
    dma = pltpu.SemaphoreType.DMA
    here, wide, _ = noise.shape
    steps, rows = here * SECTIONS, wide // SECTIONS
    vmem = pl.BlockSpec(memory_space=pltpu.VMEM)
    anywhere = pl.BlockSpec(memory_space=pl.ANY)
    V = pltpu.VMEM
    sums = (2, TILES, 8, LANES)
    return pl.pallas_call(
        window_kernel,
        in_specs=[anywhere] * 3 + [vmem] * 8,
        out_specs=[anywhere] * 2 + [vmem] * 2,
        out_shape=[
            jax.ShapeDtypeStruct(noise.shape, F32),
            jax.ShapeDtypeStruct(noise.shape, F32),
            jax.ShapeDtypeStruct(sums, F32),
            jax.ShapeDtypeStruct((8, LANES), F32),
        ],
        scratch_shapes=[
            *(V((steps, rows, L), F32) for _ in range(4)),
            V((steps, rows, L), BF), V((steps, rows, H), BF), V((steps, rows, H), BF), V((steps, rows, L), F32),
            V((here, rows, H), BF), V((here, rows, H), BF), V((here, rows, L), BF), V((here, rows, L), BF),
            V((2, 8, H), F32), V((2, 8, L), F32), V((rows, L), F32),
            V((L, H), BF), V((H, L), BF), V((L, H), BF), V((H, L), BF),
            V(sums, F32),
            V((TILES, 8, LANES), F32),
            *(V((COLORS, 3, max(SIZES) // SIDE ** (p + 1), 8, LANES), F32) for p in range(3)),
            dma((3,)), dma, dma((SECTIONS,)), dma((FINE * here,)), dma, dma((SECTIONS,)), dma, dma, dma, dma,
            dma((COLORS,)), dma((COLORS,)),
            dma((COLORS, 6, 3)), dma((COLORS, 6, 3)),
            dma((COLORS, 4)), dma((COLORS, 4)),
        ],
        name="sde_window",
        compiler_params=pltpu.CompilerParams(
            collective_id=0, has_side_effects=True, vmem_limit_bytes=62 * 1024 * 1024,
        ),
    )(start, noise, cot, *params)


def finish_kernel(
    states, adjoints, di, do, ni, no, drift_bias, noise_bias, factor,
    states_out, adjoints_out, di_out, dh_out, do_out, dof_out, ni_out, nh_out, no_out, nof_out,
):
    states_out[...] = states[...]
    adjoints_out[...] = adjoints[...]
    scale = factor[...]

    def spread(tiles, matrix):
        rows, columns = matrix.shape
        wide = columns // LANES
        for i in range(rows // 8):
            for j in range(wide):
                matrix[8 * i : 8 * i + 8, j * LANES : (j + 1) * LANES] = tiles[0, i * wide + j] * scale

    spread(di, di_out)
    spread(do, do_out)
    spread(ni, ni_out)
    spread(no, no_out)
    for tiles, hidden, last in ((drift_bias, dh_out, dof_out), (noise_bias, nh_out, nof_out)):
        for out, tile in ((hidden, tiles[0, 0] * scale), (last, tiles[0, 1] * scale)):
            for j in range(out.shape[1] // LANES):
                out[:, j * LANES : (j + 1) * LANES] = tile[j : j + 1, :]


def finish(states, adjoints, summed, factor):
    here, wide, _ = states.shape
    pieces = INNER // (INNER // here)
    tiles = INNER // pieces
    bias = 2 * INNER // tiles

    def matrix(net, base):
        return pl.BlockSpec((1, tiles, 8, LANES), lambda g: (net, base // tiles + g, 0, 0))

    def biases(net):
        return pl.BlockSpec((1, tiles, 8, LANES), lambda g: (net, bias, 0, 0))

    part = pl.BlockSpec((1, wide, L), lambda g: (g, 0, 0))
    inner = pl.BlockSpec((L // pieces, H), lambda g: (g, 0))
    outer = pl.BlockSpec((H // pieces, L), lambda g: (g, 0))

    def row(width):
        return pl.BlockSpec((1, width), lambda g: (0, 0))

    def shape(*dims):
        return jax.ShapeDtypeStruct(dims, F32)

    results = pl.pallas_call(
        finish_kernel,
        grid=(pieces,),
        in_specs=[
            part, part, matrix(0, 0), matrix(0, INNER), matrix(1, 0), matrix(1, INNER), biases(0), biases(1),
            pl.BlockSpec((8, LANES), lambda g: (0, 0)),
        ],
        out_specs=[part, part] + [inner, row(H), outer, row(L)] * 2,
        out_shape=[shape(*states.shape)] * 2 + [shape(L, H), shape(1, H), shape(H, L), shape(1, L)] * 2,
        name="sde_finish",
    )(states, adjoints, *(summed,) * 6, factor)
    return tuple(r.reshape(-1) if r.shape[0] == 1 else r for r in results)


def clip_factor(total):
    limit = 0.5 * math.sqrt(4 * L * H + 2 * H + 2 * L)
    return jnp.minimum(1.0, limit / jnp.sqrt(total))


def shards(
    initial_state, increments, cotangents,
    drift_inner, drift_hidden, drift_outer, drift_offset,
    noise_inner, noise_hidden, noise_outer, noise_offset,
):
    states, adjoints, summed, factor = window(
        initial_state,
        increments,
        cotangents,
        (
            drift_inner, drift_hidden[None], drift_outer, drift_offset[None],
            noise_inner, noise_hidden[None], noise_outer, noise_offset[None],
        ),
    )

    return finish(states, adjoints, summed, factor)


def solution(mesh):
    split = P("tm", "batch", None)
    return jax.shard_map(
        shards,
        mesh=mesh,
        in_specs=(P("batch", None), split, split) + (P(),) * 8,
        out_specs=(split, split) + (P(),) * 8,
        check_vma=False,
    )
```

```python
import math

import jax
import jax.numpy as jnp
from jax import lax
from jax.experimental import pallas as pl
from jax.experimental.pallas import tpu as pltpu
from jax.sharding import PartitionSpec as P

L = 256
H = 1024
CHUNKS = 4
SECTIONS = 8
NOISE_AT = (-1, 5, 3, 8, -1, 2, 8, 16)
COT_AT = (16, 24, 40, 32, 24, 16, -1, -1)
FINE = 2
delta_time = 0.05
LANES = 128
INNER = L * H // (8 * LANES)
COLORS = 5
SIZES = (128, 128, 128, 128, 64)
STARTS = (0, 128, 256, 384, 512)
ORDERS = ((1, 2, 0), (2, 1, 0), (1, 2, 0), (2, 1, 0), (0, 1, 2))
EARLY, LATE = (0, 1), (2, 3, 4)
SIDE = 4
TILES = sum(SIZES)
MESH = pl.DeviceIdType.MESH
F32 = jnp.float32
BF = jnp.bfloat16


def matmul(left, right):
    return jnp.dot(left, right, preferred_element_type=F32)


def matmul_rows(left, right):
    return lax.dot_general(left, right, (((0,), (0,)), ((), ())), preferred_element_type=F32)


def window_kernel(
    start, noise_hbm, cot_hbm, di, dh, do, dof, ni, nh, no, nof,
    states_hbm, adjoints_hbm, out, factor,
    noise, cot, states, adjoints, q_all, u_all, v_all, s_all,
    pb_all, rb_all, fb_all, gb_all, bias_hidden, bias_out, begin,
    dot_, dit, not_, nit, grads, held, landed1, landed2, landed3,
    own, noise_send, noise_recv, fine_recv, cot_send, cot_recv, states_send, states_recv, adj_send, adj_recv,
    sib_send, sib_recv, send, recv, back_send, back_recv,
):
    tm = lax.axis_index("tm")
    batch = lax.axis_index("batch")
    core = lax.rem(tm, 2)
    place = (lax.div(tm, 2), lax.div(batch, SIDE), lax.rem(batch, SIDE))
    other = 1 - core
    sibling = (tm + 1 - 2 * core, batch)
    here = noise_hbm.shape[0]
    rows = noise_hbm.shape[1] // SECTIONS
    total_steps = here * SECTIONS
    chunk = H // CHUNKS

    def partner(axis, distance):
        moved = lax.rem(place[axis] + distance, SIDE)
        x, y, z = (moved if a == axis else place[a] for a in range(3))
        return (2 * x + core, SIDE * y + z)

    def pick(table):
        chosen = jnp.int32(table[0])
        for index in range(1, len(table)):
            chosen = jnp.where(tm == index, table[index], chosen)
        return chosen

    def strip(index):
        return pl.ds(pl.multiple_of(index * rows, rows), rows)

    def remote(src, dst, send_sem, recv_sem, device):
        copy = pltpu.make_async_remote_copy(
            src_ref=src, dst_ref=dst, send_sem=send_sem, recv_sem=recv_sem, device_id=device, device_id_type=MESH
        )
        copy.start()
        return copy

    def local(src, dst, sem):
        copy = pltpu.make_async_copy(src, dst, sem)
        copy.start()
        return copy

    def wait_bytes(view, sem):
        pltpu.make_async_copy(view, view, sem).wait()

    begin_copy = local(start.at[strip(tm)], begin, own.at[0])

    mine = pl.ds(tm * here, here)

    @pl.when(tm < FINE)
    def _():
        def own_noise(m, _):
            k = tm * here + m
            local(noise_hbm.at[m, strip(tm)], noise.at[k], fine_recv.at[k])
            return 0

        lax.fori_loop(0, here, own_noise, 0)

    @pl.when(tm >= FINE)
    def _():
        local(noise_hbm.at[:, strip(tm)], noise.at[mine], noise_recv.at[tm])

    local(cot_hbm.at[:, strip(tm)], cot.at[mine], cot_recv.at[tm])

    barrier = pltpu.get_barrier_semaphore()
    for distance in range(1, SECTIONS):
        pl.semaphore_signal(
            barrier, inc=1, device_id=(lax.rem(tm + distance, SECTIONS), batch), device_id_type=MESH
        )
    for axis in (1, 2):
        for distance in range(1, SIDE):
            pl.semaphore_signal(barrier, inc=1, device_id=partner(axis, distance), device_id_type=MESH)
    pl.semaphore_wait(barrier, 13)

    def send_noise():
        @pl.when(tm < FINE)
        def _():
            def each(m, _):
                k = tm * here + m
                for distance in range(1, SECTIONS):
                    to = lax.rem(tm + distance, SECTIONS)
                    remote(noise_hbm.at[m, strip(to)], noise.at[k], noise_send, fine_recv.at[k], (to, batch))
                return 0

            lax.fori_loop(0, here, each, 0)

        @pl.when(tm >= FINE)
        def _():
            for distance in range(1, SECTIONS):
                to = lax.rem(tm + distance, SECTIONS)
                remote(noise_hbm.at[:, strip(to)], noise.at[mine], noise_send, noise_recv.at[tm], (to, batch))

    def send_cot():
        for distance in range(1, SECTIONS):
            to = lax.rem(tm + distance, SECTIONS)
            remote(cot_hbm.at[:, strip(to)], cot.at[mine], cot_send, cot_recv.at[tm], (to, batch))

    noise_at = pick(NOISE_AT)
    cot_at = pick(COT_AT)

    @pl.when(noise_at < 0)
    def _():
        send_noise()

    @pl.when(cot_at < 0)
    def _():
        send_cot()

    def send_states(to):
        @pl.when(to != tm)
        def _():
            remote(
                states.at[pl.ds(to * here, here)], states_hbm.at[:, strip(tm)], states_send, states_recv, (to, batch)
            )

    dot_[...] = do[...].T
    not_[...] = no[...].T
    dit[...] = di[...].T
    nit[...] = ni[...].T
    grads[...] = jnp.zeros_like(grads)
    bias_hidden[...] = jnp.zeros_like(bias_hidden)
    bias_out[...] = jnp.zeros_like(bias_out)
    begin_copy.wait()

    def sends(k):
        @pl.when(k == noise_at)
        def _():
            send_noise()

        @pl.when(k == cot_at)
        def _():
            send_cot()

    def forward_step(k, z):
        q = z.astype(BF)
        q_all[k] = q
        u = jnp.tanh(matmul(q, di[...]) + dh[...]).astype(BF)
        v = jnp.tanh(matmul(q, ni[...]) + nh[...]).astype(BF)
        u_all[k] = u
        v_all[k] = v
        drift = matmul(u, do[...])
        s = jax.nn.sigmoid(matmul(v, no[...]) + nof[...])
        s_all[k] = s
        z = z + delta_time * (drift + dof[...]) + s * noise[k]
        states[k] = z
        return z

    def fine_step(k, z):
        sends(k)
        wait_bytes(noise.at[k], fine_recv.at[k])
        return forward_step(k, z)

    def forward_section(g, z):
        sends(g * here)

        @pl.when(g == SECTIONS - 4)
        def _():
            send_states(0)
            send_states(1)

        @pl.when(g == SECTIONS - 2)
        def _():
            send_states(2)
            send_states(3)

        wait_bytes(noise.at[pl.ds(g * here, here)], noise_recv.at[g])
        return lax.fori_loop(0, here, lambda m, z: forward_step(g * here + m, z), z)

    z = lax.fori_loop(0, FINE * here, fine_step, begin[...])
    lax.fori_loop(FINE, SECTIONS, forward_section, z)

    local(states.at[mine], states_hbm.at[:, strip(tm)], own.at[1])

    def fold(x):
        return jnp.sum(x.reshape(x.shape[0] // 8, 8, x.shape[1]), 0)

    def add(net, base, stride, value):
        for h in range(2):
            part = value[:, h * LANES : (h + 1) * LANES].reshape(chunk // 8, 8, LANES)
            at = pl.ds(base + h, chunk // 8, stride=stride)
            grads[net, at] = grads[net, at] + part

    def backward_section(t, e):
        g = SECTIONS - 1 - t
        section = pl.ds(g * here, here)

        @pl.when(t < SECTIONS // 2 - 2)
        def _():
            send_states(2 * t + 4)
            send_states(2 * t + 5)

        wait_bytes(cot.at[section], cot_recv.at[g])

        def step(back, e):
            m = here - 1 - back
            k = g * here + m
            w = e + cot[k]
            s = s_all[k]
            f = delta_time * w
            r0 = w * noise[k] * s * (1.0 - s)
            fb, gb = f.astype(BF), r0.astype(BF)
            fb_all[m] = fb
            gb_all[m] = gb
            bias_out[0] += fold(f)
            bias_out[1] += fold(r0)
            acc = w
            for c in range(CHUNKS):
                cols = slice(c * chunk, (c + 1) * chunk)
                u = u_all[k, :, cols].astype(F32)
                v = v_all[k, :, cols].astype(F32)
                p = matmul(fb, dot_[:, cols]) * (1.0 - u * u)
                r = matmul(gb, not_[:, cols]) * (1.0 - v * v)
                pb, rb = p.astype(BF), r.astype(BF)
                pb_all[m, :, cols] = pb
                rb_all[m, :, cols] = rb
                bias_hidden[0, :, cols] += fold(p)
                bias_hidden[1, :, cols] += fold(r)
                acc = acc + matmul(pb, dit[cols, :]) + matmul(rb, nit[cols, :])
            adjoints[k] = acc
            return acc

        e = lax.fori_loop(0, here, step, e)

        flat = here * rows
        q = q_all[section].reshape(flat, L)
        fb = fb_all[...].reshape(flat, L)
        gb = gb_all[...].reshape(flat, L)
        for c in range(CHUNKS):
            cols = slice(c * chunk, (c + 1) * chunk)
            add(0, 2 * c, H // LANES, matmul_rows(q, pb_all[:, :, cols].reshape(flat, chunk)))
            add(1, 2 * c, H // LANES, matmul_rows(q, rb_all[:, :, cols].reshape(flat, chunk)))
            add(0, INNER + c * chunk // 4, L // LANES, matmul_rows(u_all[section, :, cols].reshape(flat, chunk), fb))
            add(1, INNER + c * chunk // 4, L // LANES, matmul_rows(v_all[section, :, cols].reshape(flat, chunk), gb))

        @pl.when(g == tm)
        def _():
            local(adjoints.at[mine], adjoints_hbm.at[:, strip(tm)], own.at[2])

        @pl.when(g != tm)
        def _():
            remote(adjoints.at[section], adjoints_hbm.at[:, strip(tm)], adj_send, adj_recv, (g, batch))

        return e

    lax.fori_loop(0, SECTIONS, backward_section, jnp.zeros((rows, L), F32))

    for net in range(2):
        hidden = jnp.sum(bias_hidden[net], 0, keepdims=True)
        last = jnp.sum(bias_out[net], 0, keepdims=True)
        for j in range(H // LANES):
            grads[net, 2 * INNER, j : j + 1, :] = hidden[:, j * LANES : (j + 1) * LANES]
        for j in range(L // LANES):
            grads[net, 2 * INNER + 1, j : j + 1, :] = last[:, j * LANES : (j + 1) * LANES]

    landed = (landed1, landed2, landed3)
    parts = [[size // SIDE ** (phase + 1) for phase in range(3)] for size in SIZES]

    swaps = {}
    for color in EARLY + LATE:
        span = pl.ds(STARTS[color], SIZES[color])
        swaps[color] = remote(grads.at[other, span], held.at[span], sib_send.at[color], sib_recv.at[color], sibling)

    bases = list(STARTS)
    moves = {}
    started = []

    def scatter(color, phase):
        axis, part = ORDERS[color][phase], parts[color][phase]
        span = pl.ds(bases[color], part * SIDE)
        if phase == 0:
            swaps[color].wait_recv()
            held[span] = held[span] + grads[core, span]
        else:
            for move in moves[color]:
                move.wait_recv()
            got, whole = landed[phase - 1].at[color], pl.ds(0, part * SIDE)
            held[span] = held[span] + got[0, whole] + (got[1, whole] + got[2, whole])
        moves[color] = [
            remote(
                held.at[pl.ds(bases[color] + lax.rem(place[axis] + distance, SIDE) * part, part)],
                landed[phase].at[color, distance - 1, pl.ds(0, part)],
                send.at[color, phase, distance - 1],
                recv.at[color, phase, distance - 1],
                partner(axis, distance),
            )
            for distance in range(1, SIDE)
        ]
        started.extend(moves[color])
        bases[color] = bases[color] + place[axis] * part

    def gather(color, phase):
        axis, part = ORDERS[color][phase], parts[color][phase]
        span = pl.ds(bases[color], part)
        for move in moves[color]:
            move.wait_recv()
        if phase == 2:
            whole = pl.ds(0, part)
            got = landed3.at[color]
            out[core, span] = held[span] + got[0, whole] + (got[1, whole] + got[2, whole])
        moves[color] = [
            remote(
                out.at[core, span],
                out.at[core, span],
                send.at[color, 5 - phase, distance - 1],
                recv.at[color, 5 - phase, distance - 1],
                partner(axis, distance),
            )
            for distance in range(1, SIDE)
        ]
        started.extend(moves[color])
        if phase == 0:
            started.append(
                remote(out.at[core, span], out.at[core, span], back_send.at[color, 0], back_recv.at[color, 0], sibling)
            )
        bases[color] = bases[color] - place[axis] * part

    def give_back(color):
        axis, part = ORDERS[color][0], parts[color][0]
        for distance in range(1, SIDE):
            moves[color][distance - 1].wait_recv()
            source = lax.rem(place[axis] + SIDE - distance, SIDE)
            span = pl.ds(bases[color] + source * part, part)
            started.append(
                remote(
                    out.at[core, span], out.at[core, span],
                    back_send.at[color, distance], back_recv.at[color, distance], sibling,
                )
            )

    tasks = [
        lambda c: scatter(c, 0), lambda c: scatter(c, 1), lambda c: scatter(c, 2),
        lambda c: gather(c, 2), lambda c: gather(c, 1), lambda c: gather(c, 0), give_back,
    ]
    order = ((EARLY, 0), (LATE, 0), (EARLY, 1), (EARLY, 2), (EARLY, 3), (LATE, 1), (EARLY, 4),
             (LATE, 2), (EARLY, 5), (LATE, 3), (LATE, 4), (LATE, 5), (EARLY, 6), (LATE, 6))
    for colors, task in order:
        for color in colors:
            tasks[task](color)
    for color in range(COLORS):
        axis, part = ORDERS[color][0], parts[color][0]
        for distance in range(SIDE):
            source = lax.rem(place[axis] + SIDE - distance, SIDE)
            view = out.at[other, pl.ds(STARTS[color] + source * part, part)]
            pltpu.make_async_copy(view, view, back_recv.at[color, distance]).wait()
    total = jnp.zeros((8, LANES), F32)
    step = 64

    def squares(i, total):
        a, b = out[0, pl.ds(i * step, step)], out[1, pl.ds(i * step, step)]
        return total + jnp.sum(a * a + b * b, 0)

    total = lax.fori_loop(0, TILES // step, squares, total)
    total = jnp.sum(jnp.sum(total, 1, keepdims=True), 0, keepdims=True)
    factor[...] = jnp.broadcast_to(clip_factor(total), (8, LANES))
    for move in [*swaps.values(), *started]:
        move.wait_send()
    others = pl.ds(0, total_steps - here)
    for sem in (noise_send, cot_send, states_send, adj_send):
        wait_bytes(noise.at[others], sem)
    sent_rows = pl.ds(0, rows * (SECTIONS - 1))
    wait_bytes(states_hbm.at[:, sent_rows], states_recv)
    wait_bytes(adjoints_hbm.at[:, sent_rows], adj_recv)
    wait_bytes(states.at[mine], own.at[1])
    wait_bytes(states.at[mine], own.at[2])


def window(start, noise, cot, params):
    dma = pltpu.SemaphoreType.DMA
    here, wide, _ = noise.shape
    steps, rows = here * SECTIONS, wide // SECTIONS
    vmem = pl.BlockSpec(memory_space=pltpu.VMEM)
    anywhere = pl.BlockSpec(memory_space=pl.ANY)
    V = pltpu.VMEM
    sums = (2, TILES, 8, LANES)
    return pl.pallas_call(
        window_kernel,
        in_specs=[anywhere] * 3 + [vmem] * 8,
        out_specs=[anywhere] * 2 + [vmem] * 2,
        out_shape=[
            jax.ShapeDtypeStruct(noise.shape, F32),
            jax.ShapeDtypeStruct(noise.shape, F32),
            jax.ShapeDtypeStruct(sums, F32),
            jax.ShapeDtypeStruct((8, LANES), F32),
        ],
        scratch_shapes=[
            *(V((steps, rows, L), F32) for _ in range(4)),
            V((steps, rows, L), BF), V((steps, rows, H), BF), V((steps, rows, H), BF), V((steps, rows, L), F32),
            V((here, rows, H), BF), V((here, rows, H), BF), V((here, rows, L), BF), V((here, rows, L), BF),
            V((2, 8, H), F32), V((2, 8, L), F32), V((rows, L), F32),
            V((L, H), BF), V((H, L), BF), V((L, H), BF), V((H, L), BF),
            V(sums, F32),
            V((TILES, 8, LANES), F32),
            *(V((COLORS, 3, max(SIZES) // SIDE ** (p + 1), 8, LANES), F32) for p in range(3)),
            dma((3,)), dma, dma((SECTIONS,)), dma((FINE * here,)), dma, dma((SECTIONS,)), dma, dma, dma, dma,
            dma((COLORS,)), dma((COLORS,)),
            dma((COLORS, 6, 3)), dma((COLORS, 6, 3)),
            dma((COLORS, 4)), dma((COLORS, 4)),
        ],
        name="sde_window",
        compiler_params=pltpu.CompilerParams(
            collective_id=0, has_side_effects=True, vmem_limit_bytes=62 * 1024 * 1024,
        ),
    )(start, noise, cot, *params)


def finish_kernel(
    states, adjoints, di, do, ni, no, drift_bias, noise_bias, factor,
    states_out, adjoints_out, di_out, dh_out, do_out, dof_out, ni_out, nh_out, no_out, nof_out,
):
    states_out[...] = states[...]
    adjoints_out[...] = adjoints[...]
    scale = factor[...]

    def spread(tiles, matrix):
        rows, columns = matrix.shape
        wide = columns // LANES
        for i in range(rows // 8):
            for j in range(wide):
                matrix[8 * i : 8 * i + 8, j * LANES : (j + 1) * LANES] = tiles[0, i * wide + j] * scale

    spread(di, di_out)
    spread(do, do_out)
    spread(ni, ni_out)
    spread(no, no_out)
    for tiles, hidden, last in ((drift_bias, dh_out, dof_out), (noise_bias, nh_out, nof_out)):
        for out, tile in ((hidden, tiles[0, 0] * scale), (last, tiles[0, 1] * scale)):
            for j in range(out.shape[1] // LANES):
                out[:, j * LANES : (j + 1) * LANES] = tile[j : j + 1, :]


def finish(states, adjoints, summed, factor):
    here, wide, _ = states.shape
    pieces = 2 * here
    tiles = INNER // pieces
    bias = 2 * INNER // tiles

    def matrix(net, base):
        return pl.BlockSpec((1, tiles, 8, LANES), lambda g: (net, base // tiles + g, 0, 0))

    def biases(net):
        return pl.BlockSpec((1, tiles, 8, LANES), lambda g: (net, bias, 0, 0))

    part = pl.BlockSpec((1, wide // 2, L), lambda g: (lax.div(g, 2), lax.rem(g, 2), 0))
    inner = pl.BlockSpec((L // pieces, H), lambda g: (g, 0))
    outer = pl.BlockSpec((H // pieces, L), lambda g: (g, 0))

    def row(width):
        return pl.BlockSpec((1, width), lambda g: (0, 0))

    def shape(*dims):
        return jax.ShapeDtypeStruct(dims, F32)

    results = pl.pallas_call(
        finish_kernel,
        grid=(pieces,),
        in_specs=[
            part, part, matrix(0, 0), matrix(0, INNER), matrix(1, 0), matrix(1, INNER), biases(0), biases(1),
            pl.BlockSpec((8, LANES), lambda g: (0, 0)),
        ],
        out_specs=[part, part] + [inner, row(H), outer, row(L)] * 2,
        out_shape=[shape(*states.shape)] * 2 + [shape(L, H), shape(1, H), shape(H, L), shape(1, L)] * 2,
        name="sde_finish",
    )(states, adjoints, *(summed,) * 6, factor)
    return tuple(r.reshape(-1) if r.shape[0] == 1 else r for r in results)


def clip_factor(total):
    limit = 0.5 * math.sqrt(4 * L * H + 2 * H + 2 * L)
    return jnp.minimum(1.0, limit / jnp.sqrt(total))


def shards(
    initial_state, increments, cotangents,
    drift_inner, drift_hidden, drift_outer, drift_offset,
    noise_inner, noise_hidden, noise_outer, noise_offset,
):
    states, adjoints, summed, factor = window(
        initial_state,
        increments,
        cotangents,
        (
            drift_inner, drift_hidden[None], drift_outer, drift_offset[None],
            noise_inner, noise_hidden[None], noise_outer, noise_offset[None],
        ),
    )

    return finish(states, adjoints, summed, factor)


def solution(mesh):
    split = P("tm", "batch", None)
    return jax.shard_map(
        shards,
        mesh=mesh,
        in_specs=(P("batch", None), split, split) + (P(),) * 8,
        out_specs=(split, split) + (P(),) * 8,
        check_vma=False,
    )
```
